32 devices in a mesh: grp: 2 (over x), pix: 8 (over z, y), disp: 2 (over core).
Axes of the slice: x: 2, y: 2, z: 4, core: 2. Of those that a mesh axis runs over, the one named last changes fastest.
Arguments:
- left_image: int32 [128, 1024], P(('grp', 'pix')), parts along dimension 0, may hold values from 0 to 255
- right_image: int32 [128, 1024], P(('grp', 'pix')), parts along dimension 0, may hold values from 0 to 255
- feat_weight: float32 [16, 16], replicated, may hold values from -1.5 to 1.5
- first_weight: bfloat16 [3, 3, 3, 16, 16], replicated, may hold values from -0.3125 to 0.3125
- first_bias: float32 [16], replicated, may hold values from -3 to 3
- second_weight: bfloat16 [3, 3, 3, 16, 16], replicated, may hold values from -0.3125 to 0.3125
- second_bias: float32 [16], replicated, may hold values from -3 to 3
- head_weight: float32 [16], replicated, may hold values from -1.5 to 1.5
- mask_weight: float32 [16, 144], replicated, may hold values from -1.5 to 1.5
- confidence: float32 [128, 1024], P(('grp', 'pix')), parts along dimension 0, may hold values from 0.1 to 1
Outputs:
- coarse_disparity: float32 [32, 256], P(('grp', 'pix')), parts along dimension 0
- disparity_map: float32 [128, 1024], P(('grp', 'pix')), parts along dimension 0
The draws below stay inside these ranges and needn't reach their ends.
There are 2 independent parts, one for each index of `grp`. The reference program is written for one: setup_inputs(seed, part) draws one part's arguments, and reference() takes and returns one part's arrays. A program takes and returns all parts, laid end to end along the dimension named above; an argument that names none is the same for every part. Nothing has to cross between parts.
All inputs are finite; a program needn't handle non-finite values.
Results may differ from the reference program's by a relative error of at most 0.0065.
Values may be sent and summed in bfloat16 or wider, within the bound.
No kernel may reach another device: no remote copies, remote signals or barrier semaphores. Data moves between devices by JAX's collectives and lax.ppermute only.
A program may use at most 64 MiB of HBM per device.

```python
import math
import jax
import jax.numpy as jnp
from jax import lax

CH = 16
DSP = 128
UP = 4
TV_ITERS = 8
FULL_ROWS = 64
FULL_COLS = 1024


def plant(values, stream_key, low, top_value):
    spot = [jax.random.randint(jax.random.fold_in(stream_key, axis), (), 0, length) for axis, length in enumerate(values.shape)]
    widest = values.shape.index(max(values.shape))
    beside = spot[:widest] + [(spot[widest] + 1) % values.shape[widest]] + spot[widest + 1:]
    return values.at[tuple(spot)].set(low).at[tuple(beside)].set(top_value)


def shard_levels(key, extent, shards, low, high):
    loudness = 1.0
    for axis_at, blocks in shards:
        draws = jax.random.uniform(jax.random.fold_in(jax.random.fold_in(key, 6), axis_at), (blocks,), jnp.float32, low / len(shards), high / len(shards))
        loudness = loudness * jnp.repeat(jnp.exp(draws), extent[axis_at] // blocks).reshape((-1,) + (1,) * (len(extent) - 1 - axis_at))
    return loudness


def gaussian(own_key, extent, scale, bound, kind=jnp.bfloat16):
    values = scale * jax.random.normal(own_key, extent, jnp.float32)
    return jnp.clip(values, min=-bound, max=bound).astype(kind)


def setup_inputs(seed: int = 0, part: int = 0) -> dict:
    key_list = jax.random.split(jax.random.key(seed), 11)
    part_splits = jax.random.split(jax.random.fold_in(key_list[10], part), 11)
    return {
        "left_image": plant(jax.random.randint(part_splits[0], (FULL_ROWS, FULL_COLS), 0, 256), jax.random.fold_in(part_splits[0], 1), 0, 255).astype(jnp.int32),
        "right_image": plant(jax.random.randint(part_splits[1], (FULL_ROWS, FULL_COLS), 0, 256), jax.random.fold_in(part_splits[1], 1), 0, 255).astype(jnp.int32),
        "feat_weight": gaussian(key_list[2], (UP * UP, CH), (UP * UP) ** -0.5, 1.5, jnp.float32),
        "first_weight": gaussian(key_list[3], (3, 3, 3, CH, CH), (27 * CH) ** -0.5, 0.3125),
        "first_bias": gaussian(key_list[4], (CH,), 0.5, 3.0, jnp.float32),
        "second_weight": gaussian(key_list[5], (3, 3, 3, CH, CH), (27 * CH) ** -0.5, 0.3125),
        "second_bias": gaussian(key_list[6], (CH,), 0.5, 3.0, jnp.float32),
        "head_weight": gaussian(key_list[7], (CH,), CH ** -0.5, 1.5, jnp.float32),
        "mask_weight": gaussian(key_list[8], (CH, 9 * UP * UP), CH ** -0.5, 1.5, jnp.float32),
        "confidence": jnp.clip(jnp.exp(math.log(1.0) - 2.3025851 * jax.random.uniform(part_splits[9], (FULL_ROWS, FULL_COLS), jnp.float32) ** shard_levels(part_splits[9], (FULL_ROWS, FULL_COLS), ((0, 8),), -0.2, 0.2)), 0.1, 1.0),
    }


dual_step = 0.175
primal_step = 0.7
tv_bound = 0.3
cost_scale = 8.0
mask_scale = 3.0
highest_prec = lax.Precision.HIGHEST

def features(image, feat_weight):
    pixels = image.astype(jnp.float32) / 64.0 - 2.0
    row_count = image.shape[0] // UP
    col_count = image.shape[1] // UP
    patches = pixels.reshape(row_count, UP, col_count, UP).transpose(1, 3, 0, 2).reshape(UP * UP, row_count, col_count)
    return jnp.einsum('pc,prw->crw', feat_weight.astype(jnp.float32), patches, precision=highest_prec).astype(jnp.bfloat16)

def cost_volume(left_feat, right_feat, planes):
    col_count = right_feat.shape[2]
    padded = jnp.pad(right_feat, ((0, 0), (0, 0), (DSP, 0)))

    def take_plane(plane):
        return lax.dynamic_slice_in_dim(padded, (DSP - plane).astype(jnp.int32), col_count, 2)
    shifted = jax.vmap(take_plane)(planes)
    return (left_feat.astype(jnp.float32)[None] * shifted.astype(jnp.float32)).astype(jnp.bfloat16)

def conv_ref(values, weights, bias):
    plane_count, channels, row_count, col_count = values.shape
    padded = jnp.pad(values.astype(jnp.float32), ((1, 1), (0, 0), (1, 1), (1, 1)))
    summed = jnp.zeros((plane_count, weights.shape[4], row_count, col_count), jnp.float32)
    for shift_d in range(3):
        for shift_y in range(3):
            for shift_x in range(3):
                window = padded[shift_d:shift_d + plane_count, :, shift_y:shift_y + row_count, shift_x:shift_x + col_count]
                summed = summed + jnp.einsum('dirw,io->dorw', window, weights[shift_d, shift_y, shift_x].astype(jnp.float32))
    return summed + bias.astype(jnp.float32)[None, :, None, None]

def upsample(rimmed, left_feat, mask_weight):
    row_count = rimmed.shape[0] - 2
    col_count = rimmed.shape[1]
    logits = mask_scale * jnp.tanh(jnp.einsum('ck,crw->krw', mask_weight, left_feat.astype(jnp.float32), precision=highest_prec))
    expo = jnp.exp(logits).reshape(9, UP * UP, row_count, col_count)
    mixing = expo / lax.optimization_barrier(jnp.sum(expo, 0))
    widened = jnp.pad(rimmed, ((0, 0), (1, 1)))
    neighbours = jnp.stack([widened[shift_y:shift_y + row_count, shift_x:shift_x + col_count] for shift_y in range(3) for shift_x in range(3)])
    subpixel = lax.optimization_barrier(jnp.sum(mixing * neighbours[:, None], 0))
    return subpixel.reshape(UP, UP, row_count, col_count).transpose(2, 0, 3, 1).reshape(row_count * UP, col_count * UP)

def zero_row(values):
    return jnp.zeros_like(values[:1])

def tv_iter(current, target, fidelity, global_fine, row_total, fetch_below, fetch_above):
    primal, extrap, dual_x, dual_y = current
    below_row = fetch_below(extrap)
    downward = jnp.concatenate([extrap[1:], below_row], 0)
    inside = ((global_fine >= 0) & (global_fine < row_total - 1))[:, None]
    grad_y = jnp.where(inside, downward - extrap, 0.0)
    grad_x = jnp.concatenate([extrap[:, 1:] - extrap[:, :-1], jnp.zeros_like(extrap[:, :1])], 1)
    trial_x = dual_x + dual_step * grad_x
    trial_y = dual_y + dual_step * grad_y
    shrink = jnp.maximum(1.0, jnp.sqrt(trial_x * trial_x + trial_y * trial_y) / tv_bound)
    dual_x = trial_x / shrink
    dual_y = trial_y / shrink
    above_row = fetch_above(dual_y)
    upper = jnp.concatenate([above_row, dual_y[:-1]], 0)
    left_col = jnp.concatenate([jnp.zeros_like(dual_x[:, :1]), dual_x[:, :-1]], 1)
    divergence = dual_x - left_col + dual_y - upper
    updated = (primal + primal_step * divergence + primal_step * fidelity * target) / (1.0 + primal_step * fidelity)
    return (updated, 2.0 * updated - primal, dual_x, dual_y)

def reference(left_image, right_image, feat_weight, first_weight, first_bias, second_weight, second_bias, head_weight, mask_weight, confidence):
    left_feat = features(left_image, feat_weight)
    right_feat = features(right_image, feat_weight)
    planes = jnp.arange(DSP, dtype=jnp.int32)
    volume = cost_volume(left_feat, right_feat, planes)
    hidden = jax.nn.relu(conv_ref(volume, first_weight, first_bias)).astype(jnp.bfloat16)
    second = jax.nn.relu(conv_ref(hidden, second_weight, second_bias))
    raw_score = jnp.einsum('dorw,o->drw', second, head_weight, precision=highest_prec)
    match_cost = cost_scale * jnp.tanh(raw_score)
    expo = jnp.exp(-match_cost)
    plane_frac = planes.astype(jnp.float32) / DSP
    coarse = lax.optimization_barrier(jnp.sum(expo * plane_frac[:, None, None], 0)) / lax.optimization_barrier(jnp.sum(expo, 0))
    rimmed = jnp.pad(coarse, ((1, 1), (0, 0)))
    initial = upsample(rimmed, left_feat, mask_weight)
    row_total = initial.shape[0]
    global_fine = jnp.arange(row_total, dtype=jnp.int32)
    current = (initial, initial, jnp.zeros_like(initial), jnp.zeros_like(initial))
    for step_index in range(TV_ITERS):
        current = tv_iter(current, initial, confidence, global_fine, row_total, zero_row, zero_row)
    return (coarse, current[0])
```

```python
import functools

import jax
import jax.numpy as jnp
from jax import lax
from jax.experimental import pallas as pl
from jax.experimental.pallas import tpu as pltpu
from jax.sharding import PartitionSpec as P

DSP = 128
UP = 4
TV_ITERS = 8
CH = 16

dual_step = 0.175
primal_step = 0.7
tv_bound = 0.3
cost_scale = 8.0
mask_scale = 3.0
f32 = jnp.float32
bf16 = jnp.bfloat16


def involution(pairs, pix_size, disp_size):
    perm = []
    used = set()
    for i, j in pairs:
        used |= {i, j}
        for d in range(disp_size):
            perm += [(i * disp_size + d, j * disp_size + d), (j * disp_size + d, i * disp_size + d)]
    for i in range(pix_size):
        if i not in used:
            perm += [(i * disp_size + d, i * disp_size + (d ^ 1)) for d in range(disp_size)]
    return sorted(perm)


def split3(values):
    high = values.astype(bf16)
    rest = values - high.astype(f32)
    middle = rest.astype(bf16)
    low = (rest - middle.astype(f32)).astype(bf16)
    return high, middle, low


def split3_outside(values):
    high = lax.reduce_precision(values, 8, 7)
    middle = lax.reduce_precision(values - high, 8, 7)
    low = values - high - middle
    return high.astype(bf16), middle.astype(bf16), low.astype(bf16)


def phase_matrix(transposed):
    rows = lax.broadcasted_iota(jnp.int32, (256, 256), 0)
    cols = lax.broadcasted_iota(jnp.int32, (256, 256), 1)
    if transposed:
        rows, cols = cols, rows
    return jnp.where(rows == UP * (cols % 64) + cols // 64, 1.0, 0.0).astype(bf16)


def deinterleave(values):
    perm = phase_matrix(False)
    chunks = values.shape[1] // 256
    pieces = [
        jnp.dot(values[:, 256 * j : 256 * j + 256], perm, preferred_element_type=f32)
        for j in range(chunks)
    ]
    lane = lax.broadcasted_iota(jnp.int32, (values.shape[0], 128), 1)
    phases = []
    for b in range(UP):
        tiles = []
        for t in range(chunks // 2):
            first = pieces[2 * t][:, 128 * (b // 2) : 128 * (b // 2) + 128]
            second = pieces[2 * t + 1][:, 128 * (b // 2) : 128 * (b // 2) + 128]
            if b % 2 == 0:
                second = pltpu.roll(second, 64, 1)
            else:
                first = pltpu.roll(first, 64, 1)
            tiles.append(jnp.where(lane < 64, first, second))
        phases.append(jnp.concatenate(tiles, 1))
    return phases


def interleave(phases):
    perm = phase_matrix(True)
    rows = phases[0].shape[0]
    lane = lax.broadcasted_iota(jnp.int32, (rows, 128), 1)
    outs = []
    for t in range(phases[0].shape[1] // 128):
        tiles = [phase[:, 128 * t : 128 * t + 128] for phase in phases]
        rolled = [pltpu.roll(tile, 64, 1) for tile in tiles]
        for half in range(2):
            if half == 0:
                packed = [jnp.where(lane < 64, tiles[b], rolled[b + 1]) for b in (0, 2)]
            else:
                packed = [jnp.where(lane < 64, rolled[b], tiles[b + 1]) for b in (0, 2)]
            packed = jnp.concatenate(packed, 1)
            total = None
            for part in split3(packed)[::-1]:
                moved = jnp.dot(part, perm, preferred_element_type=f32)
                total = moved if total is None else total + moved
            outs.append(total)
    return jnp.concatenate(outs, 1)


def shift_right(values):
    lane = lax.broadcasted_iota(jnp.int32, (values.shape[0], 128), 1)
    rolled = [pltpu.roll(values[:, t : t + 128], 1, 1) for t in range(0, values.shape[1], 128)]
    zero = jnp.zeros_like(rolled[0])
    return jnp.concatenate(
        [jnp.where(lane == 0, prev, now) for prev, now in zip([zero] + rolled[:-1], rolled)], 1
    )


def shift_left(values):
    lane = lax.broadcasted_iota(jnp.int32, (values.shape[0], 128), 1)
    rolled = [pltpu.roll(values[:, t : t + 128], 127, 1) for t in range(0, values.shape[1], 128)]
    zero = jnp.zeros_like(rolled[0])
    return jnp.concatenate(
        [jnp.where(lane == 127, after, now) for now, after in zip(rolled, rolled[1:] + [zero])], 1
    )


def join_taps(taps):
    size = taps.shape[0] // 3
    return (
        taps[size : 2 * size] + shift_right(taps[:size]) + shift_left(taps[2 * size :])
    )


def score_kernel(
    place_ref,
    own_ref,
    pair_ref,
    other_ref,
    project_ref,
    first_ref,
    second_ref,
    const_ref,
    total_ref,
    left_ref,
    conf_ref,
    volume,
    hidden,
    folded,
    *,
    pix_size,
    disp_size,
):
    pix = place_ref[0]
    disp = place_ref[1]
    plane_count = DSP // disp_size
    even = pix % 2 == 0
    pair = pair_ref[...].astype(f32)
    other = other_ref[...].astype(f32)
    above = jnp.where(even, other, pair)
    below = jnp.where(even, pair, other)
    gathered = jnp.concatenate([above, own_ref[...].astype(f32), below], 0).astype(bf16)
    phases = deinterleave(gathered)
    fine = own_ref.shape[0] // 3
    conf_ref[...] = jnp.concatenate(
        [
            jnp.concatenate([phase[s * 3 * fine + 2 * fine : s * 3 * fine + 3 * fine] for s in range(3)], 0)
            for phase in phases
        ],
        1,
    )
    stacked = jnp.concatenate(
        [
            phase[s * 3 * fine + img * fine : s * 3 * fine + (img + 1) * fine]
            for phase in phases
            for img in range(2)
            for s in range(3)
        ],
        0,
    )
    patches = (stacked / 64.0 - 2.0).astype(bf16)
    feats3 = jnp.dot(project_ref[...], patches, preferred_element_type=f32)
    size = feats3.shape[0] // 3
    feats = (feats3[2 * size :] + feats3[size : 2 * size]) + feats3[:size]
    half = size // 2
    rows = half // CH
    local_rows = rows // 3
    row_id = lax.broadcasted_iota(jnp.int32, (half, 1), 0) // CH + (pix - 1) * local_rows
    inside = (row_id >= 0) & (row_id < pix_size * local_rows)
    left = jnp.where(inside, feats[:half], 0.0).astype(bf16)
    right = feats[half:].astype(bf16).astype(f32)
    left_ref[...] = left
    left_wide = left.astype(f32)
    lane = lax.broadcasted_iota(jnp.int32, right.shape, 1)
    start = disp * plane_count

    def shifted_by(amount):
        return jnp.where(lane >= amount, pltpu.roll(right, amount, 1), 0.0)

    @pl.when(disp == 0)
    def _():
        volume[0:2] = jnp.zeros(volume[0:2].shape, bf16)

    @pl.when(disp > 0)
    def _():
        volume[0] = (left_wide * shifted_by(start - 2)).astype(bf16)
        volume[1] = (left_wide * shifted_by(start - 1)).astype(bf16)

    def fill(plane, moved):
        volume[plane] = (left_wide * moved).astype(bf16)
        return shift_right(moved)

    lax.fori_loop(2, plane_count + 4, fill, shifted_by(start), unroll=2)

    @pl.when(disp == disp_size - 1)
    def _():
        volume[plane_count + 2 :] = jnp.zeros((2,) + volume.shape[1:], bf16)

    hid_rows = hidden.shape[1]
    first = first_ref[...]
    first_bias = const_ref[0]

    def conv_first(t, carry):
        for window in range(hid_rows // 32):
            block = volume[pl.ds(2 * t, 4), 32 * window : 32 * window + 64, :]
            block = block.reshape(256, block.shape[2])
            taps = jnp.dot(first, block, preferred_element_type=f32)
            made = jnp.maximum(join_taps(taps) + first_bias, 0.0).astype(bf16)
            hidden[pl.ds(2 * t, 2), 32 * window : 32 * window + 32, :] = made.reshape(
                2, 32, made.shape[1]
            )
        return carry

    lax.fori_loop(0, plane_count // 2 + 1, conv_first, 0)

    @pl.when(disp == 0)
    def _():
        hidden[0] = jnp.zeros(hidden.shape[1:], bf16)

    @pl.when(disp == disp_size - 1)
    def _():
        hidden[plane_count + 1] = jnp.zeros(hidden.shape[1:], bf16)

    @pl.when(pix == 0)
    def _():
        hidden[:, :CH] = jnp.zeros((hidden.shape[0], CH, hidden.shape[2]), bf16)

    @pl.when(pix == pix_size - 1)
    def _():
        hidden[:, hid_rows - CH :] = jnp.zeros((hidden.shape[0], CH, hidden.shape[2]), bf16)

    second = second_ref[...]
    second_bias = const_ref[1]
    head = const_ref[2]

    def conv_second(t, carry):
        block = hidden[pl.ds(2 * t, 4)]
        block = block.reshape(256, block.shape[2])
        taps = jnp.dot(second, block, preferred_element_type=f32)
        made = jnp.maximum(join_taps(taps) + second_bias, 0.0) * head
        folded[t] = jnp.sum(made.reshape(8, 8, made.shape[1]), 0)
        return carry

    lax.fori_loop(0, plane_count // 2, conv_second, 0)

    score = folded[...]
    cols = score.shape[2]
    score = score.reshape(-1, cols)
    row8 = lax.broadcasted_iota(jnp.int32, (8, cols), 0)
    weight = jnp.zeros((8, cols), f32)
    moment = jnp.zeros((8, cols), f32)
    for t in range(plane_count // 2):
        part = score[8 * t : 8 * t + 8]
        raw = part + pltpu.roll(part, 4, 0)
        expo = jnp.exp(-cost_scale * jnp.tanh(raw))
        plane = (start + 2 * t + (row8 // 2) % 2).astype(f32) / DSP
        weight = weight + expo
        moment = moment + expo * plane
    weight = weight + pltpu.roll(weight, 2, 0)
    moment = moment + pltpu.roll(moment, 2, 0)
    total_ref[...] = jnp.where(row8 % 4 < 2, weight, moment)


def mixing_kernel(left_ref, mask_ref, mix_ref):
    cols = left_ref.shape[1]
    kinds = mask_ref.shape[0] // 3
    for r in range(mix_ref.shape[0]):
        logits3 = jnp.dot(
            mask_ref[...], left_ref[CH * r : CH * r + CH, :], preferred_element_type=f32
        )
        logits = (logits3[2 * kinds :] + logits3[kinds : 2 * kinds]) + logits3[:kinds]
        expo = jnp.exp(mask_scale * jnp.tanh(logits)).reshape(9, UP * UP, cols)
        mix_ref[r] = (expo / jnp.sum(expo, 0)).reshape(kinds, cols)


def refine_kernel(
    place_ref,
    own_ref,
    pair_ref,
    other_ref,
    far_ref,
    swapped_ref,
    mix_ref,
    conf_ref,
    out_ref,
    *,
    pix_size,
):
    pix = place_ref[0]
    disp = place_ref[1]
    local = own_ref.shape[0]
    even = pix % 2 == 0
    above = jnp.where(even, other_ref[...], pair_ref[...])
    below = jnp.where(even, pair_ref[...], other_ref[...])
    first_core = disp == 0
    far_below = jnp.where(first_core, far_ref[...], swapped_ref[...])
    far_above = jnp.where(first_core, swapped_ref[...], far_ref[...])
    window = [far_above[local - 1 :], above, own_ref[...], below, far_below[:1]]
    window = jnp.concatenate(window, 0)
    cols = window.shape[1]
    row_id = lax.broadcasted_iota(jnp.int32, window.shape, 0) + pix * local - local - 1
    window = jnp.where((row_id >= 0) & (row_id < pix_size * local), window, 0.0)
    moved = [shift_right(window), window, shift_left(window)]
    phases = [[] for _ in range(UP)]
    for r in range(3 * local):
        mixing = mix_ref[r]
        total = jnp.zeros((UP * UP, cols), f32)
        for k in range(9):
            near = moved[k % 3][r + k // 3 : r + k // 3 + 1]
            total = total + mixing[UP * UP * k : UP * UP * k + UP * UP] * near
        for b in range(UP):
            phases[b].append(total[UP * b : UP * b + UP])
    target = jnp.concatenate([jnp.concatenate(phase, 0) for phase in phases], 1)
    fine = target.shape[0]
    out_rows = fine // 3
    conf = conf_ref[...]
    lanes = target.shape[1]
    global_row = lax.broadcasted_iota(jnp.int32, target.shape, 0) + (pix - 1) * out_rows
    row_inside = (global_row >= 0) & (global_row < pix_size * out_rows - 1)
    local_row = lax.broadcasted_iota(jnp.int32, target.shape, 0)
    lane_id = lax.broadcasted_iota(jnp.int32, target.shape, 1)
    last_col = lane_id == lanes - 1
    anchor = primal_step * conf * target
    scale = 1.0 + primal_step * conf
    primal = target
    extrap = target
    dual_x = jnp.zeros_like(target)
    dual_y = jnp.zeros_like(target)
    for _ in range(TV_ITERS):
        downward = pltpu.roll(extrap, fine - 1, 0)
        grad_y = jnp.where(row_inside, downward - extrap, 0.0)
        ahead = jnp.concatenate([extrap[:, cols:], shift_left(extrap[:, :cols])], 1)
        grad_x = jnp.where(last_col, 0.0, ahead - extrap)
        trial_x = dual_x + dual_step * grad_x
        trial_y = dual_y + dual_step * grad_y
        shrink = jnp.maximum(1.0, jnp.sqrt(trial_x * trial_x + trial_y * trial_y) / tv_bound)
        dual_x = trial_x / shrink
        dual_y = trial_y / shrink
        upper = jnp.where(local_row == 0, 0.0, pltpu.roll(dual_y, 1, 0))
        behind = jnp.concatenate([shift_right(dual_x[:, lanes - cols :]), dual_x[:, : lanes - cols]], 1)
        divergence = dual_x - behind + dual_y - upper
        updated = (primal + primal_step * divergence + anchor) / scale
        extrap = 2.0 * updated - primal
        primal = updated
    kept = primal[out_rows : 2 * out_rows]
    out_ref[...] = interleave([kept[:, b * cols : (b + 1) * cols] for b in range(UP)])


def toeplitz(weights, order):
    moved = weights.transpose(2, 4, 0, 1, 3)
    blocks = jnp.stack(
        [
            jnp.pad(moved, ((0, 0), (0, 0), (do, 1 - do), (ro, 1 - ro), (0, 0)))
            for do in range(2)
            for ro in range(2)
        ],
        1,
    )
    taps, outs = (blocks.shape[0], blocks.shape[2])
    blocks = blocks.reshape(taps, 4, outs, -1)
    if order == "channel_last":
        return blocks.reshape(taps * 4 * outs, -1)
    return blocks.transpose(0, 2, 1, 3).reshape(taps * 4 * outs, -1)


def local(
    left_image,
    right_image,
    feat_weight,
    first_weight,
    first_bias,
    second_weight,
    second_bias,
    head_weight,
    mask_weight,
    confidence,
    *,
    pix_size,
    disp_size,
):
    both = ("pix", "disp")
    fine, width = left_image.shape
    cols = width // UP
    local_rows = fine // UP
    plane_count = DSP // disp_size
    place = jnp.stack([lax.axis_index("pix"), lax.axis_index("disp")]).astype(jnp.int32)
    swap = [(d, d ^ 1) for d in range(disp_size)]
    pairs = involution([(i, i + 1) for i in range(0, pix_size - 1, 2)], pix_size, disp_size)
    others = involution([(i, i + 1) for i in range(1, pix_size - 1, 2)], pix_size, disp_size)
    far = []
    taken = set()
    for i in range(pix_size - 2):
        a, b = (i * disp_size, (i + 2) * disp_size + 1)
        far += [(a, b), (b, a)]
        taken |= {a, b}
    spare = [n for n in range(pix_size * disp_size) if n not in taken]
    for a, b in zip(spare[::2], spare[1::2]):
        far += [(a, b), (b, a)]
    far = sorted(far)

    packed = jnp.concatenate(
        [left_image.astype(bf16), right_image.astype(bf16), confidence.astype(bf16)], 0
    )
    from_pair = lax.ppermute(packed, both, pairs)
    from_other = lax.ppermute(packed, both, others)

    first = toeplitz(first_weight, "channel_last")
    second = toeplitz(second_weight, "channel_first")
    groups = 6 * local_rows
    spread = jnp.einsum(
        "abc,gh->gcbha", feat_weight.reshape(UP, UP, CH), jnp.eye(groups, dtype=f32),
        precision=lax.Precision.HIGHEST,
    ).reshape(groups * CH, UP * groups * UP)
    project = jnp.concatenate(split3_outside(spread), 0)
    by_phase = mask_weight.reshape(CH, 9, UP, UP).transpose(1, 3, 2, 0).reshape(-1, CH)
    mask3 = jnp.concatenate(split3_outside(by_phase), 0)
    consts = jnp.stack(
        [jnp.tile(first_bias, 4), jnp.repeat(second_bias, 4), jnp.repeat(head_weight, 4)]
    )
    consts = jnp.broadcast_to(consts[:, :, None], consts.shape + (cols,))

    vmem = pl.BlockSpec(memory_space=pltpu.VMEM)
    smem = pl.BlockSpec(memory_space=pltpu.SMEM)
    total, left, conf = pl.pallas_call(
        functools.partial(score_kernel, pix_size=pix_size, disp_size=disp_size),
        out_shape=(
            jax.ShapeDtypeStruct((8, cols), f32),
            jax.ShapeDtypeStruct((3 * local_rows * CH, cols), bf16),
            jax.ShapeDtypeStruct((3 * fine, width), f32),
        ),
        in_specs=[smem] + [vmem] * 7,
        out_specs=(vmem, vmem, vmem),
        scratch_shapes=[
            pltpu.VMEM((plane_count + 4, 3 * local_rows * CH, cols), bf16),
            pltpu.VMEM((plane_count + 2, (local_rows + 2) * CH, cols), bf16),
            pltpu.VMEM((plane_count // 2, 8, cols), f32),
        ],
        compiler_params=pltpu.CompilerParams(vmem_limit_bytes=32 * 2**20),
        name="score",
    )(place, packed, from_pair, from_other, project, first, second, consts)

    total = total[:4]
    summed = total + lax.ppermute(total, "disp", swap)
    coarse = summed[local_rows:] / summed[:local_rows]
    far_rows = lax.ppermute(coarse, both, far)
    from_pair = lax.ppermute(coarse, both, pairs)
    from_other = lax.ppermute(coarse, both, others)
    swapped = lax.ppermute(far_rows, "disp", swap)
    mix = pl.pallas_call(
        mixing_kernel,
        out_shape=jax.ShapeDtypeStruct((3 * local_rows, mask_weight.shape[1], cols), f32),
        in_specs=[vmem, vmem],
        out_specs=vmem,
        name="mixing",
    )(left, mask3)
    refined = pl.pallas_call(
        functools.partial(refine_kernel, pix_size=pix_size),
        out_shape=jax.ShapeDtypeStruct((fine, width), f32),
        in_specs=[smem] + [vmem] * 7,
        out_specs=vmem,
        name="refine",
    )(place, coarse, from_pair, from_other, far_rows, swapped, mix, conf)
    return (coarse, refined)


def solution(mesh):
    rows = P(("grp", "pix"), None)
    placed = (rows, rows, P(), P(), P(), P(), P(), P(), P(), rows)
    return jax.shard_map(
        functools.partial(local, pix_size=mesh.shape["pix"], disp_size=mesh.shape["disp"]),
        mesh=mesh,
        in_specs=placed,
        out_specs=(rows, rows),
        check_vma=False,
    )
```

```python
import functools

import jax
import jax.numpy as jnp
from jax import lax
from jax.experimental import pallas as pl
from jax.experimental.pallas import tpu as pltpu
from jax.sharding import PartitionSpec as P

DSP = 128
UP = 4
TV_ITERS = 8
CH = 16

dual_step = 0.175
primal_step = 0.7
tv_bound = 0.3
cost_scale = 8.0
mask_scale = 3.0
f32 = jnp.float32
bf16 = jnp.bfloat16


def involution(pairs, pix_size, disp_size):
    perm = []
    used = set()
    for i, j in pairs:
        used |= {i, j}
        for d in range(disp_size):
            perm += [(i * disp_size + d, j * disp_size + d), (j * disp_size + d, i * disp_size + d)]
    for i in range(pix_size):
        if i not in used:
            perm += [(i * disp_size + d, i * disp_size + (d ^ 1)) for d in range(disp_size)]
    return sorted(perm)


def split3(values):
    high = values.astype(bf16)
    rest = values - high.astype(f32)
    middle = rest.astype(bf16)
    low = (rest - middle.astype(f32)).astype(bf16)
    return high, middle, low


def phase_matrix(transposed):
    rows = lax.broadcasted_iota(jnp.int32, (256, 256), 0)
    cols = lax.broadcasted_iota(jnp.int32, (256, 256), 1)
    if transposed:
        rows, cols = cols, rows
    return jnp.where(rows == UP * (cols % 64) + cols // 64, 1.0, 0.0).astype(bf16)


def deinterleave(values):
    perm = phase_matrix(False)
    chunks = values.shape[1] // 256
    pieces = [
        jnp.dot(values[:, 256 * j : 256 * j + 256], perm, preferred_element_type=f32)
        for j in range(chunks)
    ]
    lane = lax.broadcasted_iota(jnp.int32, (values.shape[0], 128), 1)
    phases = []
    for b in range(UP):
        tiles = []
        for t in range(chunks // 2):
            first = pieces[2 * t][:, 128 * (b // 2) : 128 * (b // 2) + 128]
            second = pieces[2 * t + 1][:, 128 * (b // 2) : 128 * (b // 2) + 128]
            if b % 2 == 0:
                second = pltpu.roll(second, 64, 1)
            else:
                first = pltpu.roll(first, 64, 1)
            tiles.append(jnp.where(lane < 64, first, second))
        phases.append(jnp.concatenate(tiles, 1))
    return phases


def interleave(phases):
    perm = phase_matrix(True)
    rows = phases[0].shape[0]
    lane = lax.broadcasted_iota(jnp.int32, (rows, 128), 1)
    outs = []
    for t in range(phases[0].shape[1] // 128):
        tiles = [phase[:, 128 * t : 128 * t + 128] for phase in phases]
        rolled = [pltpu.roll(tile, 64, 1) for tile in tiles]
        for half in range(2):
            if half == 0:
                packed = [jnp.where(lane < 64, tiles[b], rolled[b + 1]) for b in (0, 2)]
            else:
                packed = [jnp.where(lane < 64, rolled[b], tiles[b + 1]) for b in (0, 2)]
            packed = jnp.concatenate(packed, 1)
            total = None
            for part in split3(packed)[::-1]:
                moved = jnp.dot(part, perm, preferred_element_type=f32)
                total = moved if total is None else total + moved
            outs.append(total)
    return jnp.concatenate(outs, 1)


def shift_right(values, amount=1):
    lane = lax.broadcasted_iota(jnp.int32, (values.shape[0], 128), 1)
    rolled = [pltpu.roll(values[:, t : t + 128], amount, 1) for t in range(0, values.shape[1], 128)]
    zero = jnp.zeros_like(rolled[0])
    return jnp.concatenate(
        [jnp.where(lane < amount, prev, now) for prev, now in zip([zero] + rolled[:-1], rolled)], 1
    )


def shift_left(values):
    lane = lax.broadcasted_iota(jnp.int32, (values.shape[0], 128), 1)
    rolled = [pltpu.roll(values[:, t : t + 128], 127, 1) for t in range(0, values.shape[1], 128)]
    zero = jnp.zeros_like(rolled[0])
    return jnp.concatenate(
        [jnp.where(lane == 127, after, now) for now, after in zip(rolled, rolled[1:] + [zero])], 1
    )


def join_taps(taps):
    size = taps.shape[0] // 3
    return (
        taps[size : 2 * size] + shift_right(taps[:size]) + shift_left(taps[2 * size :])
    )


def score_kernel(
    own_ref,
    pair_ref,
    other_ref,
    project_ref,
    first_ref,
    second_ref,
    const_ref,
    total_ref,
    left_ref,
    conf_ref,
    volume,
    hidden,
    folded,
    *,
    pix_size,
    disp_size,
):
    pix = lax.axis_index("pix")
    disp = lax.axis_index("disp")
    plane_count = DSP // disp_size
    even = pix % 2 == 0
    pair = pair_ref[...].astype(f32)
    other = other_ref[...].astype(f32)
    above = jnp.where(even, other, pair)
    below = jnp.where(even, pair, other)
    gathered = jnp.concatenate([above, own_ref[...].astype(f32), below], 0).astype(bf16)
    phases = deinterleave(gathered)
    fine = own_ref.shape[0] // 3
    conf_ref[...] = jnp.concatenate(
        [
            jnp.concatenate([phase[s * 3 * fine + 2 * fine : s * 3 * fine + 3 * fine] for s in range(3)], 0)
            for phase in phases
        ],
        1,
    )
    stacked = jnp.concatenate(
        [
            phase[s * 3 * fine + img * fine : s * 3 * fine + (img + 1) * fine]
            for phase in phases
            for img in range(2)
            for s in range(3)
        ],
        0,
    )
    patches = (stacked / 64.0 - 2.0).astype(bf16)
    feats3 = jnp.dot(project_ref[...], patches, preferred_element_type=f32)
    size = feats3.shape[0] // 3
    feats = (feats3[2 * size :] + feats3[size : 2 * size]) + feats3[:size]
    half = size // 2
    rows = half // CH
    local_rows = rows // 3
    row_id = lax.broadcasted_iota(jnp.int32, (half, 1), 0) // CH + (pix - 1) * local_rows
    inside = (row_id >= 0) & (row_id < pix_size * local_rows)
    left = jnp.where(inside, feats[:half], 0.0).astype(bf16)
    right = feats[half:].astype(bf16).astype(f32)
    left_ref[...] = left
    left_wide = left.astype(f32)
    lane = lax.broadcasted_iota(jnp.int32, right.shape, 1)
    start = disp * plane_count

    def shifted_by(amount):
        return jnp.where(lane >= amount, pltpu.roll(right, amount, 1), 0.0)

    @pl.when(disp == 0)
    def _():
        volume[0:2] = jnp.zeros(volume[0:2].shape, bf16)

    @pl.when(disp > 0)
    def _():
        volume[0] = (left_wide * shifted_by(start - 2)).astype(bf16)
        volume[1] = (left_wide * shifted_by(start - 1)).astype(bf16)

    def fill(t, moved):
        for k in range(6):
            plane = moved if k == 0 else shift_right(moved, k)
            volume[2 + 6 * t + k] = (left_wide * plane).astype(bf16)
        return shift_right(moved, 6)

    lax.fori_loop(0, (plane_count + 2) // 6, fill, shifted_by(start))

    @pl.when(disp == disp_size - 1)
    def _():
        volume[plane_count + 2 :] = jnp.zeros((2,) + volume.shape[1:], bf16)

    hid_rows = hidden.shape[1]
    first = first_ref[...]
    first_bias = const_ref[0]

    def conv_first(t, carry):
        for window in range(hid_rows // 32):
            block = volume[pl.ds(2 * t, 4), 32 * window : 32 * window + 64, :]
            block = block.reshape(256, block.shape[2])
            taps = jnp.dot(first, block, preferred_element_type=f32)
            made = jnp.maximum(join_taps(taps) + first_bias, 0.0).astype(bf16)
            hidden[pl.ds(2 * t, 2), 32 * window : 32 * window + 32, :] = made.reshape(
                2, 32, made.shape[1]
            )
        return carry

    lax.fori_loop(0, plane_count // 2 + 1, conv_first, 0, unroll=3)

    @pl.when(disp == 0)
    def _():
        hidden[0] = jnp.zeros(hidden.shape[1:], bf16)

    @pl.when(disp == disp_size - 1)
    def _():
        hidden[plane_count + 1] = jnp.zeros(hidden.shape[1:], bf16)

    @pl.when(pix == 0)
    def _():
        hidden[:, :CH] = jnp.zeros((hidden.shape[0], CH, hidden.shape[2]), bf16)

    @pl.when(pix == pix_size - 1)
    def _():
        hidden[:, hid_rows - CH :] = jnp.zeros((hidden.shape[0], CH, hidden.shape[2]), bf16)

    second = second_ref[...]
    second_bias = const_ref[1]
    head = const_ref[2]

    def conv_second(t, carry):
        block = hidden[pl.ds(2 * t, 4)]
        block = block.reshape(256, block.shape[2])
        taps = jnp.dot(second, block, preferred_element_type=f32)
        made = jnp.maximum(join_taps(taps) + second_bias, 0.0) * head
        folded[t] = jnp.sum(made.reshape(8, 8, made.shape[1]), 0)
        return carry

    lax.fori_loop(0, plane_count // 2, conv_second, 0, unroll=4)

    score = folded[...]
    cols = score.shape[2]
    score = score.reshape(-1, cols)
    row8 = lax.broadcasted_iota(jnp.int32, (8, cols), 0)
    weight = jnp.zeros((8, cols), f32)
    moment = jnp.zeros((8, cols), f32)
    for t in range(plane_count // 2):
        part = score[8 * t : 8 * t + 8]
        raw = part + pltpu.roll(part, 4, 0)
        expo = jnp.exp(-cost_scale * jnp.tanh(raw))
        plane = (start + 2 * t + (row8 // 2) % 2).astype(f32) / DSP
        weight = weight + expo
        moment = moment + expo * plane
    weight = weight + pltpu.roll(weight, 2, 0)
    moment = moment + pltpu.roll(moment, 2, 0)
    total_ref[...] = jnp.where(row8 % 4 < 2, weight, moment)


def mixing_kernel(left_ref, mask_ref, mix_ref):
    cols = left_ref.shape[1]
    kinds = mask_ref.shape[0] // 3
    for r in range(mix_ref.shape[0]):
        logits3 = jnp.dot(
            mask_ref[...], left_ref[CH * r : CH * r + CH, :], preferred_element_type=f32
        )
        logits = (logits3[2 * kinds :] + logits3[kinds : 2 * kinds]) + logits3[:kinds]
        expo = jnp.exp(mask_scale * jnp.tanh(logits)).reshape(9, UP * UP, cols)
        mix_ref[r] = (expo / jnp.sum(expo, 0)).reshape(kinds, cols)


def refine_kernel(
    own_ref,
    pair_ref,
    other_ref,
    far_ref,
    swapped_ref,
    mix_ref,
    conf_ref,
    out_ref,
    *,
    pix_size,
):
    pix = lax.axis_index("pix")
    disp = lax.axis_index("disp")
    local = own_ref.shape[0]
    even = pix % 2 == 0
    above = jnp.where(even, other_ref[...], pair_ref[...])
    below = jnp.where(even, pair_ref[...], other_ref[...])
    first_core = disp == 0
    far_below = jnp.where(first_core, far_ref[...], swapped_ref[...])
    far_above = jnp.where(first_core, swapped_ref[...], far_ref[...])
    window = [far_above[local - 1 :], above, own_ref[...], below, far_below[:1]]
    window = jnp.concatenate(window, 0)
    cols = window.shape[1]
    row_id = lax.broadcasted_iota(jnp.int32, window.shape, 0) + pix * local - local - 1
    window = jnp.where((row_id >= 0) & (row_id < pix_size * local), window, 0.0)
    moved = [shift_right(window), window, shift_left(window)]
    phases = [[] for _ in range(UP)]
    for r in range(3 * local):
        mixing = mix_ref[r]
        total = jnp.zeros((UP * UP, cols), f32)
        for k in range(9):
            near = moved[k % 3][r + k // 3 : r + k // 3 + 1]
            total = total + mixing[UP * UP * k : UP * UP * k + UP * UP] * near
        for b in range(UP):
            phases[b].append(total[UP * b : UP * b + UP])
    target = jnp.concatenate([jnp.concatenate(phase, 0) for phase in phases], 1)
    fine = target.shape[0]
    out_rows = fine // 3
    conf = conf_ref[...]
    lanes = target.shape[1]
    global_row = lax.broadcasted_iota(jnp.int32, target.shape, 0) + (pix - 1) * out_rows
    row_inside = (global_row >= 0) & (global_row < pix_size * out_rows - 1)
    lane_id = lax.broadcasted_iota(jnp.int32, target.shape, 1)
    last_col = lane_id == lanes - 1
    anchor = primal_step * conf * target
    scale = 1.0 / (1.0 + primal_step * conf)
    both_steps = primal_step * dual_step
    gain_y = jnp.where(row_inside, both_steps, 0.0)
    gain_x = jnp.where(last_col, 0.0, both_steps)
    bound = primal_step * tv_bound
    primal = target
    extrap = target
    dual_x = jnp.zeros_like(target)
    dual_y = jnp.zeros_like(target)
    for _ in range(TV_ITERS):
        downward = pltpu.roll(extrap, fine - 1, 0)
        ahead = jnp.concatenate([extrap[:, cols:], shift_left(extrap[:, :cols])], 1)
        trial_x = dual_x + gain_x * (ahead - extrap)
        trial_y = dual_y + gain_y * (downward - extrap)
        shrink = jnp.minimum(1.0, bound * lax.rsqrt(trial_x * trial_x + trial_y * trial_y))
        dual_x = trial_x * shrink
        dual_y = trial_y * shrink
        upper = pltpu.roll(dual_y, 1, 0)
        behind = jnp.concatenate([shift_right(dual_x[:, lanes - cols :]), dual_x[:, : lanes - cols]], 1)
        updated = (primal + (dual_x - behind + dual_y - upper) + anchor) * scale
        extrap = 2.0 * updated - primal
        primal = updated
    kept = primal[out_rows : 2 * out_rows]
    out_ref[...] = interleave([kept[:, b * cols : (b + 1) * cols] for b in range(UP)])


def pack_kernel(left_ref, right_ref, conf_ref, out_ref):
    parts = [left_ref[...].astype(f32), right_ref[...].astype(f32), conf_ref[...]]
    out_ref[...] = jnp.concatenate(parts, 0).astype(bf16)


def transposed(values):
    size = values.shape[1]
    eye = lax.broadcasted_iota(jnp.int32, (size, size), 0) == lax.broadcasted_iota(
        jnp.int32, (size, size), 1
    )
    eye = jnp.where(eye, 1.0, 0.0).astype(bf16)
    flipped = lax.dot_general(
        eye, values, (((1,), (1,)), ((), ())), preferred_element_type=f32
    )
    return flipped.astype(bf16)


def column(values, index):
    count = values.shape[0]
    lane = lax.broadcasted_iota(jnp.int32, (index.shape[0], count), 1)
    wide = jnp.broadcast_to(values.reshape(1, count), (index.shape[0], count))
    return jnp.sum(jnp.where(lane == index, wide, 0.0), 1, keepdims=True)


def prepare_kernel(
    feat_ref,
    first_weight_ref,
    first_bias_ref,
    second_weight_ref,
    second_bias_ref,
    head_ref,
    mask_weight_ref,
    project_ref,
    first_ref,
    second_ref,
    const_ref,
    mask_ref,
):
    taps = first_weight_ref.shape[0] ** 3 * CH
    flat = [
        transposed(ref[...].reshape(taps, CH)) for ref in (first_weight_ref, second_weight_ref)
    ]
    flat = jnp.concatenate(flat, 0)
    source = lax.broadcasted_iota(jnp.int32, (taps, 256), 0)
    lane = lax.broadcasted_iota(jnp.int32, (1, 256), 1)
    plane, row, chan = (lane // 64, (lane // CH) % 4, lane % CH)
    out_row = lax.broadcasted_iota(jnp.int32, (64, 64), 0)
    out_col = lax.broadcasted_iota(jnp.int32, (64, 64), 1)
    regroup = jnp.where(out_col == (out_row % 4) * CH + out_row // 4, 1.0, 0.0).astype(bf16)
    for tap in range(3):
        wanted = jnp.where((plane < 3) & (row < 3), ((plane * 3 + row) * 3 + tap) * CH + chan, -1)
        select = jnp.where(source == wanted, 1.0, 0.0).astype(bf16)
        base = jnp.dot(flat, select, preferred_element_type=f32)
        placed = [base] + [pltpu.roll(base, 64 * (j // 2) + CH * (j % 2), 1) for j in range(1, 4)]
        blocks = [jnp.concatenate([p[n * CH : n * CH + CH] for p in placed], 0) for n in range(2)]
        first_ref[64 * tap : 64 * tap + 64, :] = blocks[0].astype(bf16)
        mixed = jnp.dot(regroup, blocks[1].astype(bf16), preferred_element_type=f32)
        second_ref[64 * tap : 64 * tap + 64, :] = mixed.astype(bf16)

    size = project_ref.shape[1]
    groups = size // (UP * UP)
    pixel = lax.broadcasted_iota(jnp.int32, (UP * UP, size), 0)
    spot = lax.broadcasted_iota(jnp.int32, (UP * UP, size), 1)
    expand = jnp.where(pixel == UP * (spot % UP) + spot // (UP * groups), 1.0, 0.0).astype(bf16)
    own_group = lax.broadcasted_iota(jnp.int32, (size, size), 0) // CH
    keep = own_group == (lax.broadcasted_iota(jnp.int32, (size, size), 1) // UP) % groups
    for n, part in enumerate(split3(feat_ref[...])):
        wide = jnp.dot(transposed(part), expand, preferred_element_type=f32)
        wide = jnp.concatenate([wide] * groups, 0)
        project_ref[size * n : size * n + size, :] = jnp.where(keep, wide, 0.0).astype(bf16)

    kinds = mask_weight_ref.shape[1]
    new = lax.broadcasted_iota(jnp.int32, (kinds, kinds), 0)
    old = lax.broadcasted_iota(jnp.int32, (kinds, kinds), 1)
    swapped = (new // (UP * UP)) * (UP * UP) + (new % UP) * UP + (new // UP) % UP
    swapped = jnp.where(old == swapped, 1.0, 0.0).astype(bf16)
    for n, part in enumerate(split3(mask_weight_ref[...])):
        moved = lax.dot_general(
            swapped, part, (((1,), (1,)), ((), ())), preferred_element_type=f32
        )
        mask_ref[kinds * n : kinds * n + kinds, :] = moved.astype(bf16)

    index = lax.broadcasted_iota(jnp.int32, (64, 1), 0)
    shape = const_ref.shape[1:]
    const_ref[0] = jnp.broadcast_to(column(first_bias_ref[...], index % CH), shape)
    const_ref[1] = jnp.broadcast_to(column(second_bias_ref[...], index // 4), shape)
    const_ref[2] = jnp.broadcast_to(column(head_ref[...], index // 4), shape)


def local(
    left_image,
    right_image,
    feat_weight,
    first_weight,
    first_bias,
    second_weight,
    second_bias,
    head_weight,
    mask_weight,
    confidence,
    *,
    pix_size,
    disp_size,
):
    both = ("pix", "disp")
    fine, width = left_image.shape
    cols = width // UP
    local_rows = fine // UP
    plane_count = DSP // disp_size
    swap = [(d, d ^ 1) for d in range(disp_size)]
    pairs = involution([(i, i + 1) for i in range(0, pix_size - 1, 2)], pix_size, disp_size)
    others = involution([(i, i + 1) for i in range(1, pix_size - 1, 2)], pix_size, disp_size)
    far = []
    taken = set()
    for i in range(pix_size - 2):
        a, b = (i * disp_size, (i + 2) * disp_size + 1)
        far += [(a, b), (b, a)]
        taken |= {a, b}
    spare = [n for n in range(pix_size * disp_size) if n not in taken]
    for a, b in zip(spare[::2], spare[1::2]):
        far += [(a, b), (b, a)]
    far = sorted(far)

    vmem = pl.BlockSpec(memory_space=pltpu.VMEM)
    packed = pl.pallas_call(
        pack_kernel,
        out_shape=jax.ShapeDtypeStruct((3 * fine, width), bf16),
        in_specs=[vmem] * 3,
        out_specs=vmem,
        compiler_params=pltpu.CompilerParams(vmem_limit_bytes=2 * 2**20),
        name="pack",
    )(left_image, right_image, confidence)
    from_pair = lax.ppermute(packed, both, pairs)
    from_other = lax.ppermute(packed, both, others)

    groups = 6 * local_rows
    kinds = mask_weight.shape[1]
    project, first, second, consts, mask3 = pl.pallas_call(
        prepare_kernel,
        out_shape=(
            jax.ShapeDtypeStruct((3 * groups * CH, groups * UP * UP), bf16),
            jax.ShapeDtypeStruct((192, 256), bf16),
            jax.ShapeDtypeStruct((192, 256), bf16),
            jax.ShapeDtypeStruct((3, 64, cols), f32),
            jax.ShapeDtypeStruct((3 * kinds, CH), bf16),
        ),
        in_specs=[vmem] * 7,
        out_specs=(vmem,) * 5,
        compiler_params=pltpu.CompilerParams(vmem_limit_bytes=8 * 2**20),
        name="prepare",
    )(
        feat_weight,
        first_weight,
        first_bias,
        second_weight,
        second_bias,
        head_weight,
        mask_weight,
    )
    total, left, conf = pl.pallas_call(
        functools.partial(score_kernel, pix_size=pix_size, disp_size=disp_size),
        out_shape=(
            jax.ShapeDtypeStruct((8, cols), f32),
            jax.ShapeDtypeStruct((3 * local_rows * CH, cols), bf16),
            jax.ShapeDtypeStruct((3 * fine, width), f32),
        ),
        in_specs=[vmem] * 7,
        out_specs=(vmem, vmem, vmem),
        scratch_shapes=[
            pltpu.VMEM((plane_count + 4, 3 * local_rows * CH, cols), bf16),
            pltpu.VMEM((plane_count + 2, (local_rows + 2) * CH, cols), bf16),
            pltpu.VMEM((plane_count // 2, 8, cols), f32),
        ],
        compiler_params=pltpu.CompilerParams(vmem_limit_bytes=16 * 2**20),
        name="score",
    )(packed, from_pair, from_other, project, first, second, consts)

    total = total[:4]
    summed = total + lax.ppermute(total, "disp", swap)
    coarse = summed[local_rows:] / summed[:local_rows]
    far_rows = lax.ppermute(coarse, both, far)
    from_pair = lax.ppermute(coarse, both, pairs)
    from_other = lax.ppermute(coarse, both, others)
    swapped = lax.ppermute(far_rows, "disp", swap)
    mix = pl.pallas_call(
        mixing_kernel,
        out_shape=jax.ShapeDtypeStruct((3 * local_rows, mask_weight.shape[1], cols), f32),
        in_specs=[vmem, vmem],
        out_specs=vmem,
        compiler_params=pltpu.CompilerParams(vmem_limit_bytes=4 * 2**20),
        name="mixing",
    )(left, mask3)
    refined = pl.pallas_call(
        functools.partial(refine_kernel, pix_size=pix_size),
        out_shape=jax.ShapeDtypeStruct((fine, width), f32),
        in_specs=[vmem] * 7,
        out_specs=vmem,
        compiler_params=pltpu.CompilerParams(vmem_limit_bytes=8 * 2**20),
        name="refine",
    )(coarse, from_pair, from_other, far_rows, swapped, mix, conf)
    return (coarse, refined)


def solution(mesh):
    rows = P(("grp", "pix"), None)
    placed = (rows, rows, P(), P(), P(), P(), P(), P(), P(), rows)
    return jax.shard_map(
        functools.partial(local, pix_size=mesh.shape["pix"], disp_size=mesh.shape["disp"]),
        mesh=mesh,
        in_specs=placed,
        out_specs=(rows, rows),
        check_vma=False,
    )
```

```python
import functools

import jax
import jax.numpy as jnp
from jax import lax
from jax.experimental import pallas as pl
from jax.experimental.pallas import tpu as pltpu
from jax.sharding import PartitionSpec as P

DSP = 128
UP = 4
TV_ITERS = 8
CH = 16

dual_step = 0.175
primal_step = 0.7
tv_bound = 0.3
cost_scale = 8.0
mask_scale = 3.0
f32 = jnp.float32
bf16 = jnp.bfloat16


def mixed_exchange(pix_size, disp_size):
    send = {}
    for i in range(pix_size):
        send[i, 0] = (i ^ 1, 0)
        j = i + 1 if i % 2 else i - 1
        send[i, 1] = (j, 1) if 0 <= j < pix_size else (i, 0)
    for end in (0, pix_size - 1):
        send[end ^ 1, 0] = (end, 1)
    order = sorted(send)
    return [tuple(p * disp_size + d for p, d in (key, send[key])) for key in order]


def sort_neighbours(received, swapped, pix, disp, pix_size):
    at_end = (pix == 0) | (pix == pix_size - 1)
    direct = (disp == 0) != at_end
    even = pix % 2 == 0
    first_is_below = direct == even
    below = jnp.where(first_is_below, received, swapped)
    above = jnp.where(first_is_below, swapped, received)
    return above, below


def split3(values):
    high = values.astype(bf16)
    rest = values - high.astype(f32)
    middle = rest.astype(bf16)
    low = (rest - middle.astype(f32)).astype(bf16)
    return high, middle, low


def phase_matrix(transposed):
    rows = lax.broadcasted_iota(jnp.int32, (256, 256), 0)
    cols = lax.broadcasted_iota(jnp.int32, (256, 256), 1)
    if transposed:
        rows, cols = cols, rows
    return jnp.where(rows == UP * (cols % 64) + cols // 64, 1.0, 0.0).astype(bf16)


def deinterleave(values):
    perm = phase_matrix(False)
    chunks = values.shape[1] // 256
    pieces = [
        jnp.dot(values[:, 256 * j : 256 * j + 256], perm, preferred_element_type=f32)
        for j in range(chunks)
    ]
    lane = lax.broadcasted_iota(jnp.int32, (values.shape[0], 128), 1)
    phases = []
    for b in range(UP):
        tiles = []
        for t in range(chunks // 2):
            first = pieces[2 * t][:, 128 * (b // 2) : 128 * (b // 2) + 128]
            second = pieces[2 * t + 1][:, 128 * (b // 2) : 128 * (b // 2) + 128]
            if b % 2 == 0:
                second = pltpu.roll(second, 64, 1)
            else:
                first = pltpu.roll(first, 64, 1)
            tiles.append(jnp.where(lane < 64, first, second))
        phases.append(jnp.concatenate(tiles, 1))
    return phases


def interleave(phases):
    perm = phase_matrix(True)
    rows = phases[0].shape[0]
    lane = lax.broadcasted_iota(jnp.int32, (rows, 128), 1)
    outs = []
    for t in range(phases[0].shape[1] // 128):
        tiles = [phase[:, 128 * t : 128 * t + 128] for phase in phases]
        rolled = [pltpu.roll(tile, 64, 1) for tile in tiles]
        for half in range(2):
            if half == 0:
                packed = [jnp.where(lane < 64, tiles[b], rolled[b + 1]) for b in (0, 2)]
            else:
                packed = [jnp.where(lane < 64, rolled[b], tiles[b + 1]) for b in (0, 2)]
            packed = jnp.concatenate(packed, 1)
            total = None
            for part in split3(packed)[::-1]:
                moved = jnp.dot(part, perm, preferred_element_type=f32)
                total = moved if total is None else total + moved
            outs.append(total)
    return jnp.concatenate(outs, 1)


def shift_right(values, amount=1):
    lane = lax.broadcasted_iota(jnp.int32, (values.shape[0], 128), 1)
    rolled = [pltpu.roll(values[:, t : t + 128], amount, 1) for t in range(0, values.shape[1], 128)]
    zero = jnp.zeros_like(rolled[0])
    return jnp.concatenate(
        [jnp.where(lane < amount, prev, now) for prev, now in zip([zero] + rolled[:-1], rolled)], 1
    )


def shift_left(values):
    lane = lax.broadcasted_iota(jnp.int32, (values.shape[0], 128), 1)
    rolled = [pltpu.roll(values[:, t : t + 128], 127, 1) for t in range(0, values.shape[1], 128)]
    zero = jnp.zeros_like(rolled[0])
    return jnp.concatenate(
        [jnp.where(lane == 127, after, now) for now, after in zip(rolled, rolled[1:] + [zero])], 1
    )


def join_taps(taps):
    size = taps.shape[0] // 3
    sides = shift_right(taps[:size].astype(bf16)) + shift_left(taps[2 * size :].astype(bf16))
    return taps[size : 2 * size] + sides.astype(f32)


def score_kernel(
    own_ref,
    received_ref,
    exchanged_ref,
    project_ref,
    first_ref,
    second_ref,
    const_ref,
    total_ref,
    left_ref,
    conf_ref,
    volume,
    hidden,
    *,
    pix_size,
    disp_size,
):
    pix = lax.axis_index("pix")
    disp = lax.axis_index("disp")
    plane_count = DSP // disp_size
    above, below = sort_neighbours(
        received_ref[...].astype(f32), exchanged_ref[...].astype(f32), pix, disp, pix_size
    )
    gathered = jnp.concatenate([above, own_ref[...].astype(f32), below], 0).astype(bf16)
    phases = deinterleave(gathered)
    fine = own_ref.shape[0] // 3
    conf_ref[...] = jnp.concatenate(
        [
            jnp.concatenate([phase[s * 3 * fine + 2 * fine : s * 3 * fine + 3 * fine] for s in range(3)], 0)
            for phase in phases
        ],
        1,
    )
    stacked = jnp.concatenate(
        [
            phase[s * 3 * fine + img * fine : s * 3 * fine + (img + 1) * fine]
            for phase in phases
            for img in range(2)
            for s in range(3)
        ],
        0,
    )
    patches = (stacked / 64.0 - 2.0).astype(bf16)
    feats3 = jnp.dot(project_ref[...], patches, preferred_element_type=f32)
    size = feats3.shape[0] // 3
    feats = (feats3[2 * size :] + feats3[size : 2 * size]) + feats3[:size]
    half = size // 2
    rows = half // CH
    local_rows = rows // 3
    row_id = lax.broadcasted_iota(jnp.int32, (half, 1), 0) // CH + (pix - 1) * local_rows
    inside = (row_id >= 0) & (row_id < pix_size * local_rows)
    left = jnp.where(inside, feats[:half], 0.0).astype(bf16)
    right = feats[half:].astype(bf16).astype(f32)
    left_ref[...] = left
    lane = lax.broadcasted_iota(jnp.int32, right.shape, 1)
    start = disp * plane_count

    def shifted_by(amount):
        return jnp.where(lane >= amount, pltpu.roll(right, amount, 1), 0.0).astype(bf16)

    hid_rows, cols = hidden.shape[1:]
    windows = hid_rows // 32
    pair_count = plane_count // 2 + 1
    state = [shifted_by(start)]

    def fill(t):
        if t == 0:
            planes = [shifted_by(jnp.maximum(start - 2 + k, 0)) for k in range(2)]
            planes = [jnp.where(disp > 0, plane, jnp.zeros_like(plane)) for plane in planes]
        else:
            base = state[-1]
            step = 2 * ((t - 1) % 3)
            planes = [base if step + k == 0 else shift_right(base, step + k) for k in range(2)]
            if step == 4:
                state.append(shift_right(base, 6))
            if t == pair_count:
                exists = disp < disp_size - 1
                planes = [jnp.where(exists, plane, jnp.zeros_like(plane)) for plane in planes]
        for k in range(2):
            volume[2 * t + k] = left * planes[k]

    block_row = lax.broadcasted_iota(jnp.int32, (first_ref.shape[0], 1), 0) // CH
    live = [block_row >= 0 for _ in range(windows)]
    live[0] = (pix > 0) | (block_row % 2 == 1)
    live[-1] = live[-1] & ((pix < pix_size - 1) | (block_row % 2 == 0))
    first = [jnp.where(keep, first_ref[...].astype(f32), 0.0).astype(bf16) for keep in live]
    first_bias = [jnp.where(keep[:64], const_ref[0], 0.0) for keep in live]

    def conv_first(t):
        for window in range(windows):
            block = volume[2 * t : 2 * t + 4, 32 * window : 32 * window + 64, :]
            taps = jnp.dot(first[window], block.reshape(256, cols), preferred_element_type=f32)
            made = jnp.maximum(join_taps(taps) + first_bias[window], 0.0)
            halves = [made[:32], made[32:]]
            if t == 0:
                halves[0] = jnp.where(disp > 0, halves[0], 0.0)
            if t == pair_count - 1:
                halves[1] = jnp.where(disp < disp_size - 1, halves[1], 0.0)
            for k in range(2):
                hidden[2 * t + k, 32 * window : 32 * window + 32, :] = halves[k].astype(bf16)

    second = second_ref[...]
    second_bias = const_ref[1]
    head = const_ref[2]
    partial = []

    def conv_second(t):
        block = hidden[2 * t : 2 * t + 4]
        taps = jnp.dot(second, block.reshape(256, cols), preferred_element_type=f32)
        made = jnp.maximum(join_taps(taps) + second_bias, 0.0) * head
        partial.append(jnp.sum(made.reshape(8, 8, cols), 0))

    for t in range(pair_count + 1):
        fill(t)
    for t in range(pair_count):
        conv_first(t)
    for t in range(pair_count - 1):
        conv_second(t)

    row8 = lax.broadcasted_iota(jnp.int32, (8, cols), 0)
    weight = jnp.zeros((8, cols), f32)
    moment = jnp.zeros((8, cols), f32)
    for t in range(plane_count // 2):
        part = partial[t]
        raw = part + pltpu.roll(part, 4, 0)
        expo = jnp.exp(-cost_scale * jnp.tanh(raw))
        plane = (start + 2 * t + (row8 // 2) % 2).astype(f32) / DSP
        weight = weight + expo
        moment = moment + expo * plane
    weight = weight + pltpu.roll(weight, 2, 0)
    moment = moment + pltpu.roll(moment, 2, 0)
    total_ref[...] = jnp.where(row8 % 4 < 2, weight, moment)


def mixing_kernel(left_ref, mask_ref, mix_ref):
    cols = left_ref.shape[1]
    kinds = mask_ref.shape[0] // 3
    for r in range(mix_ref.shape[0]):
        logits3 = jnp.dot(
            mask_ref[...], left_ref[CH * r : CH * r + CH, :], preferred_element_type=f32
        )
        logits = (logits3[2 * kinds :] + logits3[kinds : 2 * kinds]) + logits3[:kinds]
        expo = jnp.exp(mask_scale * jnp.tanh(logits)).reshape(9, UP * UP, cols)
        mix_ref[r] = (expo / jnp.sum(expo, 0)).reshape(kinds, cols)


def refine_kernel(
    own_ref,
    received_ref,
    exchanged_ref,
    far_ref,
    swapped_ref,
    mix_ref,
    conf_ref,
    out_ref,
    *,
    pix_size,
):
    pix = lax.axis_index("pix")
    disp = lax.axis_index("disp")
    local = own_ref.shape[0]
    above, below = sort_neighbours(received_ref[...], exchanged_ref[...], pix, disp, pix_size)
    first_core = disp == 0
    far_below = jnp.where(first_core, far_ref[...], swapped_ref[...])
    far_above = jnp.where(first_core, swapped_ref[...], far_ref[...])
    window = [far_above[local - 1 :], above, own_ref[...], below, far_below[:1]]
    window = jnp.concatenate(window, 0)
    cols = window.shape[1]
    row_id = lax.broadcasted_iota(jnp.int32, window.shape, 0) + pix * local - local - 1
    window = jnp.where((row_id >= 0) & (row_id < pix_size * local), window, 0.0)
    moved = [shift_right(window), window, shift_left(window)]
    phases = [[] for _ in range(UP)]
    for r in range(3 * local):
        mixing = mix_ref[r]
        total = jnp.zeros((UP * UP, cols), f32)
        for k in range(9):
            near = moved[k % 3][r + k // 3 : r + k // 3 + 1]
            total = total + mixing[UP * UP * k : UP * UP * k + UP * UP] * near
        for b in range(UP):
            phases[b].append(total[UP * b : UP * b + UP])
    target = jnp.concatenate([jnp.concatenate(phase, 0) for phase in phases], 1)
    fine = target.shape[0]
    out_rows = fine // 3
    conf = conf_ref[...]
    lanes = target.shape[1]
    global_row = lax.broadcasted_iota(jnp.int32, target.shape, 0) + (pix - 1) * out_rows
    row_inside = (global_row >= 0) & (global_row < pix_size * out_rows - 1)
    target = target * (dual_step / tv_bound)
    anchor = primal_step * conf * target
    scale = 1.0 / (1.0 + primal_step * conf)
    keep_y = jnp.where(row_inside, 1.0, 0.0)
    last_lane = lax.broadcasted_iota(jnp.int32, (fine, cols), 1) == cols - 1
    primal = target
    extrap = target
    dual_x = None
    for _ in range(TV_ITERS):
        trial_y = keep_y * (pltpu.roll(extrap, fine - 1, 0) - extrap)
        wrapped = jnp.where(last_lane, extrap[:, lanes - cols :], shift_left(extrap[:, :cols]))
        trial_x = jnp.concatenate([extrap[:, cols:], wrapped], 1) - extrap
        if dual_x is not None:
            trial_x = dual_x + trial_x
            trial_y = dual_y + trial_y
        shrink = lax.rsqrt(jnp.maximum(1.0, trial_x * trial_x + trial_y * trial_y))
        dual_x = trial_x * shrink
        dual_y = trial_y * shrink
        upper = pltpu.roll(dual_y, 1, 0)
        behind = jnp.concatenate([shift_right(dual_x[:, lanes - cols :]), dual_x[:, : lanes - cols]], 1)
        divergence = dual_x - behind + dual_y - upper
        updated = (primal + (primal_step * dual_step) * divergence + anchor) * scale
        extrap = 2.0 * updated - primal
        primal = updated
    primal = primal * (tv_bound / dual_step)
    kept = primal[out_rows : 2 * out_rows]
    out_ref[...] = interleave([kept[:, b * cols : (b + 1) * cols] for b in range(UP)])


def in_hbm(values):
    return pltpu.with_memory_space_constraint(values, pltpu.HBM)


def pack_kernel(left_ref, right_ref, conf_ref, out_ref, images, conf, sems):
    copies = [
        pltpu.make_async_copy(left_ref, images.at[0], sems.at[0]),
        pltpu.make_async_copy(right_ref, images.at[1], sems.at[1]),
        pltpu.make_async_copy(conf_ref, conf, sems.at[2]),
    ]
    for copy in copies:
        copy.start()
    for copy in copies:
        copy.wait()
    parts = [images[0].astype(f32), images[1].astype(f32), conf[...]]
    out_ref[...] = jnp.concatenate(parts, 0).astype(bf16)


def transposed(values):
    size = values.shape[1]
    eye = lax.broadcasted_iota(jnp.int32, (size, size), 0) == lax.broadcasted_iota(
        jnp.int32, (size, size), 1
    )
    eye = jnp.where(eye, 1.0, 0.0).astype(bf16)
    flipped = lax.dot_general(
        eye, values, (((1,), (1,)), ((), ())), preferred_element_type=f32
    )
    return flipped.astype(bf16)


def column(values, index):
    count = values.shape[0]
    lane = lax.broadcasted_iota(jnp.int32, (index.shape[0], count), 1)
    wide = jnp.broadcast_to(values.reshape(1, count), (index.shape[0], count))
    return jnp.sum(jnp.where(lane == index, wide, 0.0), 1, keepdims=True)


def prepare_kernel(
    feat_ref,
    first_weight_ref,
    first_bias_ref,
    second_weight_ref,
    second_bias_ref,
    head_ref,
    mask_weight_ref,
    project_ref,
    first_ref,
    second_ref,
    const_ref,
    mask_ref,
    weights,
    sems,
):
    copies = [
        pltpu.make_async_copy(ref, weights.at[n], sems.at[n])
        for n, ref in enumerate((first_weight_ref, second_weight_ref))
    ]
    for copy in copies:
        copy.start()

    size = project_ref.shape[1]
    groups = size // (UP * UP)
    pixel = lax.broadcasted_iota(jnp.int32, (UP * UP, size), 0)
    spot = lax.broadcasted_iota(jnp.int32, (UP * UP, size), 1)
    expand = jnp.where(pixel == UP * (spot % UP) + spot // (UP * groups), 1.0, 0.0).astype(bf16)
    own_group = lax.broadcasted_iota(jnp.int32, (size, size), 0) // CH
    keep = own_group == (lax.broadcasted_iota(jnp.int32, (size, size), 1) // UP) % groups
    for n, part in enumerate(split3(feat_ref[...])):
        wide = jnp.dot(transposed(part), expand, preferred_element_type=f32)
        wide = jnp.concatenate([wide] * groups, 0)
        project_ref[size * n : size * n + size, :] = jnp.where(keep, wide, 0.0).astype(bf16)

    kinds = mask_weight_ref.shape[1]
    new = lax.broadcasted_iota(jnp.int32, (kinds, kinds), 0)
    old = lax.broadcasted_iota(jnp.int32, (kinds, kinds), 1)
    swapped = (new // (UP * UP)) * (UP * UP) + (new % UP) * UP + (new // UP) % UP
    swapped = jnp.where(old == swapped, 1.0, 0.0).astype(bf16)
    for n, part in enumerate(split3(mask_weight_ref[...])):
        moved = lax.dot_general(
            swapped, part, (((1,), (1,)), ((), ())), preferred_element_type=f32
        )
        mask_ref[kinds * n : kinds * n + kinds, :] = moved.astype(bf16)

    index = lax.broadcasted_iota(jnp.int32, (64, 1), 0)
    shape = const_ref.shape[1:]
    const_ref[0] = jnp.broadcast_to(column(first_bias_ref[...], index % CH), shape)
    const_ref[1] = jnp.broadcast_to(column(second_bias_ref[...], index // 4), shape)
    const_ref[2] = jnp.broadcast_to(column(head_ref[...], index // 4), shape)

    for copy in copies:
        copy.wait()
    taps = weights.shape[1] ** 3 * CH
    flat = [transposed(weights[n].reshape(taps, CH)) for n in range(2)]
    flat = jnp.concatenate(flat, 0)
    source = lax.broadcasted_iota(jnp.int32, (taps, 256), 0)
    lane = lax.broadcasted_iota(jnp.int32, (1, 256), 1)
    plane, row, chan = (lane // 64, (lane // CH) % 4, lane % CH)
    out_row = lax.broadcasted_iota(jnp.int32, (64, 64), 0)
    out_col = lax.broadcasted_iota(jnp.int32, (64, 64), 1)
    regroup = jnp.where(out_col == (out_row % 4) * CH + out_row // 4, 1.0, 0.0).astype(bf16)
    for tap in range(3):
        wanted = jnp.where((plane < 3) & (row < 3), ((plane * 3 + row) * 3 + tap) * CH + chan, -1)
        select = jnp.where(source == wanted, 1.0, 0.0).astype(bf16)
        base = jnp.dot(flat, select, preferred_element_type=f32)
        placed = [base] + [pltpu.roll(base, 64 * (j // 2) + CH * (j % 2), 1) for j in range(1, 4)]
        blocks = [jnp.concatenate([p[n * CH : n * CH + CH] for p in placed], 0) for n in range(2)]
        first_ref[64 * tap : 64 * tap + 64, :] = blocks[0].astype(bf16)
        mixed = jnp.dot(regroup, blocks[1].astype(bf16), preferred_element_type=f32)
        second_ref[64 * tap : 64 * tap + 64, :] = mixed.astype(bf16)


def local(
    left_image,
    right_image,
    feat_weight,
    first_weight,
    first_bias,
    second_weight,
    second_bias,
    head_weight,
    mask_weight,
    confidence,
    *,
    pix_size,
    disp_size,
):
    both = ("pix", "disp")
    fine, width = left_image.shape
    cols = width // UP
    local_rows = fine // UP
    plane_count = DSP // disp_size
    swap = [(d, d ^ 1) for d in range(disp_size)]
    neighbours = mixed_exchange(pix_size, disp_size)
    far = []
    taken = set()
    for i in range(pix_size - 2):
        a, b = (i * disp_size, (i + 2) * disp_size + 1)
        far += [(a, b), (b, a)]
        taken |= {a, b}
    spare = [n for n in range(pix_size * disp_size) if n not in taken]
    for a, b in zip(spare[::2], spare[1::2]):
        far += [(a, b), (b, a)]
    far = sorted(far)

    vmem = pl.BlockSpec(memory_space=pltpu.VMEM)
    hbm = pl.BlockSpec(memory_space=pltpu.HBM)
    packed = pl.pallas_call(
        pack_kernel,
        out_shape=jax.ShapeDtypeStruct((3 * fine, width), bf16),
        in_specs=[hbm] * 3,
        out_specs=vmem,
        scratch_shapes=[
            pltpu.VMEM((2, fine, width), left_image.dtype),
            pltpu.VMEM((fine, width), f32),
            pltpu.SemaphoreType.DMA((3,)),
        ],
        compiler_params=pltpu.CompilerParams(vmem_limit_bytes=2 * 2**20),
        name="pack",
    )(in_hbm(left_image), in_hbm(right_image), in_hbm(confidence))
    received = lax.ppermute(packed, both, neighbours)

    groups = 6 * local_rows
    kinds = mask_weight.shape[1]
    project, first, second, consts, mask3 = pl.pallas_call(
        prepare_kernel,
        out_shape=(
            jax.ShapeDtypeStruct((3 * groups * CH, groups * UP * UP), bf16),
            jax.ShapeDtypeStruct((192, 256), bf16),
            jax.ShapeDtypeStruct((192, 256), bf16),
            jax.ShapeDtypeStruct((3, 64, cols), f32),
            jax.ShapeDtypeStruct((3 * kinds, CH), bf16),
        ),
        in_specs=[vmem, hbm, vmem, hbm, vmem, vmem, vmem],
        out_specs=(vmem,) * 5,
        scratch_shapes=[
            pltpu.VMEM((2,) + first_weight.shape, bf16),
            pltpu.SemaphoreType.DMA((2,)),
        ],
        compiler_params=pltpu.CompilerParams(vmem_limit_bytes=8 * 2**20),
        name="prepare",
    )(
        feat_weight,
        in_hbm(first_weight),
        first_bias,
        in_hbm(second_weight),
        second_bias,
        head_weight,
        mask_weight,
    )
    received, project, first, second, consts, mask3 = lax.optimization_barrier(
        (received, project, first, second, consts, mask3)
    )
    exchanged = lax.ppermute(received, "disp", swap)
    total, left, conf = pl.pallas_call(
        functools.partial(score_kernel, pix_size=pix_size, disp_size=disp_size),
        out_shape=(
            jax.ShapeDtypeStruct((8, cols), f32),
            jax.ShapeDtypeStruct((3 * local_rows * CH, cols), bf16),
            jax.ShapeDtypeStruct((3 * fine, width), f32),
        ),
        in_specs=[vmem] * 7,
        out_specs=(vmem, vmem, vmem),
        scratch_shapes=[
            pltpu.VMEM((plane_count + 4, 3 * local_rows * CH, cols), bf16),
            pltpu.VMEM((plane_count + 2, (local_rows + 2) * CH, cols), bf16),
        ],
        compiler_params=pltpu.CompilerParams(vmem_limit_bytes=16 * 2**20),
        name="score",
    )(packed, received, exchanged, project, first, second, consts)

    total = total[:4]
    summed = total + lax.ppermute(total, "disp", swap)
    coarse = summed[local_rows:] / summed[:local_rows]
    received = lax.ppermute(coarse, both, neighbours)
    far_rows = lax.ppermute(coarse, both, far)
    exchanged = lax.ppermute(received, "disp", swap)
    swapped = lax.ppermute(far_rows, "disp", swap)
    mix = pl.pallas_call(
        mixing_kernel,
        out_shape=jax.ShapeDtypeStruct((3 * local_rows, mask_weight.shape[1], cols), f32),
        in_specs=[vmem, vmem],
        out_specs=vmem,
        compiler_params=pltpu.CompilerParams(vmem_limit_bytes=4 * 2**20),
        name="mixing",
    )(left, mask3)
    refined = pl.pallas_call(
        functools.partial(refine_kernel, pix_size=pix_size),
        out_shape=jax.ShapeDtypeStruct((fine, width), f32),
        in_specs=[vmem] * 7,
        out_specs=vmem,
        compiler_params=pltpu.CompilerParams(vmem_limit_bytes=8 * 2**20),
        name="refine",
    )(coarse, received, exchanged, far_rows, swapped, mix, conf)
    return (coarse, refined)


def solution(mesh):
    rows = P(("grp", "pix"), None)
    placed = (rows, rows, P(), P(), P(), P(), P(), P(), P(), rows)
    return jax.shard_map(
        functools.partial(local, pix_size=mesh.shape["pix"], disp_size=mesh.shape["disp"]),
        mesh=mesh,
        in_specs=placed,
        out_specs=(rows, rows),
        check_vma=False,
    )
```

```python
import functools

import jax
import jax.numpy as jnp
from jax import lax
from jax.experimental import pallas as pl
from jax.experimental.pallas import tpu as pltpu
from jax.sharding import PartitionSpec as P

DSP = 128
UP = 4
TV_ITERS = 8
CH = 16

dual_step = 0.175
primal_step = 0.7
tv_bound = 0.3
cost_scale = 8.0
mask_scale = 3.0
f32 = jnp.float32
bf16 = jnp.bfloat16


def involution(pairs, pix_size, disp_size):
    perm = []
    used = set()
    for i, j in pairs:
        used |= {i, j}
        for d in range(disp_size):
            perm += [(i * disp_size + d, j * disp_size + d), (j * disp_size + d, i * disp_size + d)]
    for i in range(pix_size):
        if i not in used:
            perm += [(i * disp_size + d, i * disp_size + (d ^ 1)) for d in range(disp_size)]
    return sorted(perm)


def mixed_exchange(pix_size, disp_size):
    send = {}
    for i in range(pix_size):
        send[i, 0] = (i ^ 1, 0)
        j = i + 1 if i % 2 else i - 1
        send[i, 1] = (j, 1) if 0 <= j < pix_size else (i, 0)
    for end in (0, pix_size - 1):
        send[end ^ 1, 0] = (end, 1)
    order = sorted(send)
    return [tuple(p * disp_size + d for p, d in (key, send[key])) for key in order]


def sort_neighbours(received, swapped, pix, disp, pix_size):
    at_end = (pix == 0) | (pix == pix_size - 1)
    direct = (disp == 0) != at_end
    even = pix % 2 == 0
    first_is_below = direct == even
    below = jnp.where(first_is_below, received, swapped)
    above = jnp.where(first_is_below, swapped, received)
    return above, below


def split3(values):
    high = values.astype(bf16)
    rest = values - high.astype(f32)
    middle = rest.astype(bf16)
    low = (rest - middle.astype(f32)).astype(bf16)
    return high, middle, low


def phase_matrix(transposed):
    rows = lax.broadcasted_iota(jnp.int32, (256, 256), 0)
    cols = lax.broadcasted_iota(jnp.int32, (256, 256), 1)
    if transposed:
        rows, cols = cols, rows
    return jnp.where(rows == UP * (cols & 63) + (cols >> 6), 1.0, 0.0).astype(bf16)


def deinterleave(values):
    perm = phase_matrix(False)
    chunks = values.shape[1] // 256
    pieces = [
        jnp.dot(values[:, 256 * j : 256 * j + 256], perm, preferred_element_type=f32)
        for j in range(chunks)
    ]
    lane = lax.broadcasted_iota(jnp.int32, (values.shape[0], 128), 1)
    phases = []
    for b in range(UP):
        tiles = []
        for t in range(chunks // 2):
            first = pieces[2 * t][:, 128 * (b // 2) : 128 * (b // 2) + 128]
            second = pieces[2 * t + 1][:, 128 * (b // 2) : 128 * (b // 2) + 128]
            if b % 2 == 0:
                second = pltpu.roll(second, 64, 1)
            else:
                first = pltpu.roll(first, 64, 1)
            tiles.append(jnp.where(lane < 64, first, second))
        phases.append(jnp.concatenate(tiles, 1))
    return phases


def interleave(phases):
    rows = phases[0].shape[0]
    lane = lax.broadcasted_iota(jnp.int32, (rows, 128), 1)
    chunks = []
    for t in range(phases[0].shape[1] // 128):
        tiles = [phase[:, 128 * t : 128 * t + 128] for phase in phases]
        rolled = [pltpu.roll(tile, 64, 1) for tile in tiles]
        chunks.append([jnp.where(lane < 64, tiles[b], rolled[b + 1]) for b in (0, 2)])
        chunks.append([jnp.where(lane < 64, rolled[b], tiles[b + 1]) for b in (0, 2)])
    packed = jnp.concatenate([jnp.concatenate(chunk, 1) for chunk in chunks], 0)
    size = packed.shape[0]
    parts = jnp.concatenate(split3(packed), 0)
    moved = jnp.dot(parts, phase_matrix(True), preferred_element_type=f32)
    moved = (moved[2 * size :] + moved[size : 2 * size]) + moved[:size]
    return jnp.concatenate([moved[rows * j : rows * j + rows] for j in range(len(chunks))], 1)


def shift_right(values, amount=1):
    lane = lax.broadcasted_iota(jnp.int32, (values.shape[0], 128), 1)
    rolled = [pltpu.roll(values[:, t : t + 128], amount, 1) for t in range(0, values.shape[1], 128)]
    zero = jnp.zeros_like(rolled[0])
    return jnp.concatenate(
        [jnp.where(lane < amount, prev, now) for prev, now in zip([zero] + rolled[:-1], rolled)], 1
    )


def shift_left(values):
    lane = lax.broadcasted_iota(jnp.int32, (values.shape[0], 128), 1)
    rolled = [pltpu.roll(values[:, t : t + 128], 127, 1) for t in range(0, values.shape[1], 128)]
    zero = jnp.zeros_like(rolled[0])
    return jnp.concatenate(
        [jnp.where(lane == 127, after, now) for now, after in zip(rolled, rolled[1:] + [zero])], 1
    )


def join_taps(taps):
    size = taps.shape[0] // 3
    sides = shift_right(taps[:size].astype(bf16)) + shift_left(taps[2 * size :].astype(bf16))
    return taps[size : 2 * size] + sides.astype(f32)


def score_kernel(
    own_ref,
    received_ref,
    exchanged_ref,
    project_ref,
    first_ref,
    second_ref,
    const_ref,
    total_ref,
    left_ref,
    conf_ref,
    volume,
    hidden,
    *,
    pix_size,
    disp_size,
):
    pix = lax.axis_index("pix")
    disp = lax.axis_index("disp")
    plane_count = DSP // disp_size
    even = pix % 2 == 0
    pair, other = (received_ref[...].astype(f32), exchanged_ref[...].astype(f32))
    above = jnp.where(even, other, pair)
    below = jnp.where(even, pair, other)
    gathered = jnp.concatenate([above, own_ref[...].astype(f32), below], 0).astype(bf16)
    phases = deinterleave(gathered)
    fine = own_ref.shape[0] // 3
    conf_ref[...] = jnp.concatenate(
        [
            jnp.concatenate([phase[s * 3 * fine + 2 * fine : s * 3 * fine + 3 * fine] for s in range(3)], 0)
            for phase in phases
        ],
        1,
    )
    stacked = jnp.concatenate(
        [
            phase[s * 3 * fine + img * fine : s * 3 * fine + (img + 1) * fine]
            for phase in phases
            for img in range(2)
            for s in range(3)
        ],
        0,
    )
    patches = (stacked / 64.0 - 2.0).astype(bf16)
    feats3 = jnp.dot(project_ref[...], patches, preferred_element_type=f32)
    size = feats3.shape[0] // 3
    feats = (feats3[2 * size :] + feats3[size : 2 * size]) + feats3[:size]
    half = size // 2
    rows = half // CH
    local_rows = rows // 3
    row_id = lax.broadcasted_iota(jnp.int32, (half, 1), 0) // CH + (pix - 1) * local_rows
    inside = (row_id >= 0) & (row_id < pix_size * local_rows)
    left = jnp.where(inside, feats[:half], 0.0).astype(bf16)
    right = feats[half:].astype(bf16).astype(f32)
    left_ref[...] = left
    lane = lax.broadcasted_iota(jnp.int32, right.shape, 1)
    start = disp * plane_count

    def shifted_by(amount):
        return jnp.where(lane >= amount, pltpu.roll(right, amount, 1), 0.0).astype(bf16)

    hid_rows, cols = hidden.shape[1:]
    windows = hid_rows // 32
    pair_count = plane_count // 2 + 1
    state = [shifted_by(start)]

    def fill(t):
        if t == 0:
            planes = [shifted_by(jnp.maximum(start - 2 + k, 0)) for k in range(2)]
            planes = [jnp.where(disp > 0, plane, jnp.zeros_like(plane)) for plane in planes]
        else:
            base = state[-1]
            step = 2 * ((t - 1) % 3)
            planes = [base if step + k == 0 else shift_right(base, step + k) for k in range(2)]
            if step == 4:
                state.append(shift_right(base, 6))
            if t == pair_count:
                exists = disp < disp_size - 1
                planes = [jnp.where(exists, plane, jnp.zeros_like(plane)) for plane in planes]
        for k in range(2):
            volume[2 * t + k] = left * planes[k]

    block_row = lax.broadcasted_iota(jnp.int32, (first_ref.shape[0], 1), 0) // CH
    live = [block_row >= 0 for _ in range(windows)]
    live[0] = (pix > 0) | ((block_row & 1) == 1)
    live[-1] = live[-1] & ((pix < pix_size - 1) | ((block_row & 1) == 0))
    first = [jnp.where(keep, first_ref[...].astype(f32), 0.0).astype(bf16) for keep in live]
    first_bias = [jnp.where(keep[:64], const_ref[0], 0.0) for keep in live]

    def conv_first(t):
        for window in range(windows):
            block = volume[2 * t : 2 * t + 4, 32 * window : 32 * window + 64, :]
            taps = jnp.dot(first[window], block.reshape(256, cols), preferred_element_type=f32)
            made = jnp.maximum(join_taps(taps) + first_bias[window], 0.0)
            halves = [made[:32], made[32:]]
            if t == 0:
                halves[0] = jnp.where(disp > 0, halves[0], 0.0)
            if t == pair_count - 1:
                halves[1] = jnp.where(disp < disp_size - 1, halves[1], 0.0)
            for k in range(2):
                hidden[2 * t + k, 32 * window : 32 * window + 32, :] = halves[k].astype(bf16)

    second = second_ref[...]
    second_bias = const_ref[1]
    head = const_ref[2]
    partial = []

    def conv_second(t):
        block = hidden[2 * t : 2 * t + 4]
        taps = jnp.dot(second, block.reshape(256, cols), preferred_element_type=f32)
        made = jnp.maximum(join_taps(taps) + second_bias, 0.0) * head
        partial.append(jnp.sum(made.reshape(8, 8, cols), 0))

    for t in range(pair_count + 1):
        fill(t)
    for t in range(pair_count):
        conv_first(t)
    for t in range(pair_count - 1):
        conv_second(t)

    row8 = lax.broadcasted_iota(jnp.int32, (8, cols), 0)
    weight = jnp.zeros((8, cols), f32)
    moment = jnp.zeros((8, cols), f32)
    upper = row8 < 4
    for t in range(0, plane_count // 2, 2):
        kept = jnp.where(upper, partial[t], partial[t + 1])
        other = jnp.where(upper, partial[t + 1], partial[t])
        raw = kept + pltpu.roll(other, 4, 0)
        expo = jnp.exp(-cost_scale * jnp.tanh(raw))
        plane = (start + 2 * t + (row8 >> 1)).astype(f32) / DSP
        weight = weight + expo
        moment = moment + expo * plane
    for turn in (4, 2):
        weight = weight + pltpu.roll(weight, turn, 0)
        moment = moment + pltpu.roll(moment, turn, 0)
    total_ref[...] = jnp.where((row8 & 3) < 2, weight, moment)


def mixing_kernel(left_ref, mask_weight_ref, mix_ref):
    cols = left_ref.shape[1]
    kinds = mask_weight_ref.shape[1]
    new = lax.broadcasted_iota(jnp.int32, (kinds, kinds), 0)
    old = lax.broadcasted_iota(jnp.int32, (kinds, kinds), 1)
    swapped = (new & ~15) + (new & 3) * UP + ((new >> 2) & 3)
    swapped = jnp.where(old == swapped, 1.0, 0.0).astype(bf16)
    mask = jnp.concatenate(
        [
            lax.dot_general(
                swapped, part, (((1,), (1,)), ((), ())), preferred_element_type=f32
            ).astype(bf16)
            for part in split3(mask_weight_ref[...])
        ],
        0,
    )
    for r in range(mix_ref.shape[0]):
        logits3 = jnp.dot(mask, left_ref[CH * r : CH * r + CH, :], preferred_element_type=f32)
        logits = (logits3[2 * kinds :] + logits3[kinds : 2 * kinds]) + logits3[:kinds]
        expo = jnp.exp(mask_scale * jnp.tanh(logits)).reshape(9, UP * UP, cols)
        mix_ref[r] = (expo / jnp.sum(expo, 0)).reshape(kinds, cols)


def refine_kernel(
    own_ref,
    received_ref,
    exchanged_ref,
    far_ref,
    swapped_ref,
    mix_ref,
    conf_ref,
    out_ref,
    *,
    pix_size,
):
    pix = lax.axis_index("pix")
    disp = lax.axis_index("disp")
    local = own_ref.shape[0]
    above, below = sort_neighbours(received_ref[...], exchanged_ref[...], pix, disp, pix_size)
    first_core = disp == 0
    far_below = jnp.where(first_core, far_ref[...], swapped_ref[...])
    far_above = jnp.where(first_core, swapped_ref[...], far_ref[...])
    window = [far_above[local - 1 :], above, own_ref[...], below, far_below[:1]]
    window = jnp.concatenate(window, 0)
    cols = window.shape[1]
    row_id = lax.broadcasted_iota(jnp.int32, window.shape, 0) + pix * local - local - 1
    window = jnp.where((row_id >= 0) & (row_id < pix_size * local), window, 0.0)
    moved = [shift_right(window), window, shift_left(window)]
    phases = [[] for _ in range(UP)]
    for r in range(3 * local):
        mixing = mix_ref[r]
        total = jnp.zeros((UP * UP, cols), f32)
        for k in range(9):
            near = moved[k % 3][r + k // 3 : r + k // 3 + 1]
            total = total + mixing[UP * UP * k : UP * UP * k + UP * UP] * near
        for b in range(UP):
            phases[b].append(total[UP * b : UP * b + UP])
    target = jnp.concatenate([jnp.concatenate(phase, 0) for phase in phases], 1)
    fine = target.shape[0]
    out_rows = fine // 3
    conf = conf_ref[...]
    lanes = target.shape[1]
    global_row = lax.broadcasted_iota(jnp.int32, target.shape, 0) + (pix - 1) * out_rows
    row_inside = (global_row >= 0) & (global_row < pix_size * out_rows - 1)
    target = target * (dual_step / tv_bound)
    anchor = primal_step * conf * target
    scale = 1.0 / (1.0 + primal_step * conf)
    keep_y = jnp.where(row_inside, 1.0, 0.0)
    last_lane = lax.broadcasted_iota(jnp.int32, (fine, cols), 1) == cols - 1
    primal = target
    extrap = target
    dual_x = None
    for _ in range(TV_ITERS):
        trial_y = keep_y * (pltpu.roll(extrap, fine - 1, 0) - extrap)
        wrapped = jnp.where(last_lane, extrap[:, lanes - cols :], shift_left(extrap[:, :cols]))
        trial_x = jnp.concatenate([extrap[:, cols:], wrapped], 1) - extrap
        if dual_x is not None:
            trial_x = dual_x + trial_x
            trial_y = dual_y + trial_y
        shrink = lax.rsqrt(jnp.maximum(1.0, trial_x * trial_x + trial_y * trial_y))
        dual_x = trial_x * shrink
        dual_y = trial_y * shrink
        upper = pltpu.roll(dual_y, 1, 0)
        behind = jnp.concatenate([shift_right(dual_x[:, lanes - cols :]), dual_x[:, : lanes - cols]], 1)
        divergence = dual_x - behind + dual_y - upper
        updated = (primal + (primal_step * dual_step) * divergence + anchor) * scale
        extrap = 2.0 * updated - primal
        primal = updated
    primal = primal * (tv_bound / dual_step)
    kept = primal[out_rows : 2 * out_rows]
    out_ref[...] = interleave([kept[:, b * cols : (b + 1) * cols] for b in range(UP)])


def in_hbm(values):
    return pltpu.with_memory_space_constraint(values, pltpu.HBM)


def pack_kernel(left_ref, right_ref, conf_ref, out_ref, images, conf, sems):
    copies = [
        pltpu.make_async_copy(left_ref, images.at[0], sems.at[0]),
        pltpu.make_async_copy(right_ref, images.at[1], sems.at[1]),
        pltpu.make_async_copy(conf_ref, conf, sems.at[2]),
    ]
    for copy in copies:
        copy.start()
    for copy in copies:
        copy.wait()
    parts = [images[0].astype(f32), images[1].astype(f32), conf[...]]
    out_ref[...] = jnp.concatenate(parts, 0).astype(bf16)


def transposed(values):
    size = values.shape[1]
    eye = lax.broadcasted_iota(jnp.int32, (size, size), 0) == lax.broadcasted_iota(
        jnp.int32, (size, size), 1
    )
    eye = jnp.where(eye, 1.0, 0.0).astype(bf16)
    flipped = lax.dot_general(
        eye, values, (((1,), (1,)), ((), ())), preferred_element_type=f32
    )
    return flipped.astype(bf16)


def column(values, index):
    count = values.shape[0]
    lane = lax.broadcasted_iota(jnp.int32, (index.shape[0], count), 1)
    wide = jnp.broadcast_to(values.reshape(1, count), (index.shape[0], count))
    return jnp.sum(jnp.where(lane == index, wide, 0.0), 1, keepdims=True)


def prepare_kernel(
    feat_ref,
    first_weight_ref,
    first_bias_ref,
    second_weight_ref,
    second_bias_ref,
    head_ref,
    project_ref,
    first_ref,
    second_ref,
    const_ref,
    weights,
    sems,
):
    copies = [
        pltpu.make_async_copy(ref, weights.at[n], sems.at[n])
        for n, ref in enumerate((first_weight_ref, second_weight_ref))
    ]
    for copy in copies:
        copy.start()

    size = project_ref.shape[1]
    groups = size // (UP * UP)
    pixel = lax.broadcasted_iota(jnp.int32, (UP * UP, size), 0)
    spot = lax.broadcasted_iota(jnp.int32, (UP * UP, size), 1)
    expand = jnp.where(pixel == UP * (spot % UP) + spot // (UP * groups), 1.0, 0.0).astype(bf16)
    own_group = lax.broadcasted_iota(jnp.int32, (size, size), 0) // CH
    keep = own_group == (lax.broadcasted_iota(jnp.int32, (size, size), 1) // UP) % groups
    for n, part in enumerate(split3(feat_ref[...])):
        wide = jnp.dot(transposed(part), expand, preferred_element_type=f32)
        wide = jnp.concatenate([wide] * groups, 0)
        project_ref[size * n : size * n + size, :] = jnp.where(keep, wide, 0.0).astype(bf16)

    index = lax.broadcasted_iota(jnp.int32, (64, 1), 0)
    shape = const_ref.shape[1:]
    const_ref[0] = jnp.broadcast_to(column(first_bias_ref[...], index % CH), shape)
    const_ref[1] = jnp.broadcast_to(column(second_bias_ref[...], index // 4), shape)
    const_ref[2] = jnp.broadcast_to(column(head_ref[...], index // 4), shape)

    for copy in copies:
        copy.wait()
    taps = weights.shape[1] ** 3 * CH
    flat = [transposed(weights[n].reshape(taps, CH)) for n in range(2)]
    flat = jnp.concatenate(flat, 0)
    source = lax.broadcasted_iota(jnp.int32, (taps, 256), 0)
    lane = lax.broadcasted_iota(jnp.int32, (1, 256), 1)
    plane, row, chan = (lane >> 6, (lane >> 4) & 3, lane & 15)
    out_row = lax.broadcasted_iota(jnp.int32, (64, 64), 0)
    out_col = lax.broadcasted_iota(jnp.int32, (64, 64), 1)
    regroup = jnp.where(out_col == (out_row & 3) * CH + (out_row >> 2), 1.0, 0.0).astype(bf16)
    for tap in range(3):
        wanted = jnp.where((plane < 3) & (row < 3), ((plane * 3 + row) * 3 + tap) * CH + chan, -1)
        select = jnp.where(source == wanted, 1.0, 0.0).astype(bf16)
        base = jnp.dot(flat, select, preferred_element_type=f32)
        placed = [base] + [pltpu.roll(base, 64 * (j // 2) + CH * (j % 2), 1) for j in range(1, 4)]
        blocks = [jnp.concatenate([p[n * CH : n * CH + CH] for p in placed], 0) for n in range(2)]
        first_ref[64 * tap : 64 * tap + 64, :] = blocks[0].astype(bf16)
        mixed = jnp.dot(regroup, blocks[1].astype(bf16), preferred_element_type=f32)
        second_ref[64 * tap : 64 * tap + 64, :] = mixed.astype(bf16)


def local(
    left_image,
    right_image,
    feat_weight,
    first_weight,
    first_bias,
    second_weight,
    second_bias,
    head_weight,
    mask_weight,
    confidence,
    *,
    pix_size,
    disp_size,
):
    both = ("pix", "disp")
    fine, width = left_image.shape
    cols = width // UP
    local_rows = fine // UP
    plane_count = DSP // disp_size
    swap = [(d, d ^ 1) for d in range(disp_size)]
    neighbours = mixed_exchange(pix_size, disp_size)
    pairs = involution([(i, i + 1) for i in range(0, pix_size - 1, 2)], pix_size, disp_size)
    others = involution([(i, i + 1) for i in range(1, pix_size - 1, 2)], pix_size, disp_size)
    far = []
    taken = set()
    for i in range(pix_size - 2):
        a, b = (i * disp_size, (i + 2) * disp_size + 1)
        far += [(a, b), (b, a)]
        taken |= {a, b}
    spare = [n for n in range(pix_size * disp_size) if n not in taken]
    for a, b in zip(spare[::2], spare[1::2]):
        far += [(a, b), (b, a)]
    far = sorted(far)

    vmem = pl.BlockSpec(memory_space=pltpu.VMEM)
    hbm = pl.BlockSpec(memory_space=pltpu.HBM)
    packed = pl.pallas_call(
        pack_kernel,
        out_shape=jax.ShapeDtypeStruct((3 * fine, width), bf16),
        in_specs=[hbm] * 3,
        out_specs=vmem,
        scratch_shapes=[
            pltpu.VMEM((2, fine, width), left_image.dtype),
            pltpu.VMEM((fine, width), f32),
            pltpu.SemaphoreType.DMA((3,)),
        ],
        compiler_params=pltpu.CompilerParams(vmem_limit_bytes=2 * 2**20),
        name="pack",
    )(in_hbm(left_image), in_hbm(right_image), in_hbm(confidence))
    from_pair = lax.ppermute(packed, both, pairs)
    from_other = lax.ppermute(packed, both, others)

    groups = 6 * local_rows
    project, first, second, consts = pl.pallas_call(
        prepare_kernel,
        out_shape=(
            jax.ShapeDtypeStruct((3 * groups * CH, groups * UP * UP), bf16),
            jax.ShapeDtypeStruct((192, 256), bf16),
            jax.ShapeDtypeStruct((192, 256), bf16),
            jax.ShapeDtypeStruct((3, 64, cols), f32),
        ),
        in_specs=[vmem, hbm, vmem, hbm, vmem, vmem],
        out_specs=(vmem,) * 4,
        scratch_shapes=[
            pltpu.VMEM((2,) + first_weight.shape, bf16),
            pltpu.SemaphoreType.DMA((2,)),
        ],
        compiler_params=pltpu.CompilerParams(vmem_limit_bytes=8 * 2**20),
        name="prepare",
    )(
        feat_weight,
        in_hbm(first_weight),
        first_bias,
        in_hbm(second_weight),
        second_bias,
        head_weight,
    )
    total, left, conf = pl.pallas_call(
        functools.partial(score_kernel, pix_size=pix_size, disp_size=disp_size),
        out_shape=(
            jax.ShapeDtypeStruct((8, cols), f32),
            jax.ShapeDtypeStruct((3 * local_rows * CH, cols), bf16),
            jax.ShapeDtypeStruct((3 * fine, width), f32),
        ),
        in_specs=[vmem] * 7,
        out_specs=(vmem, vmem, vmem),
        scratch_shapes=[
            pltpu.VMEM((plane_count + 4, 3 * local_rows * CH, cols), bf16),
            pltpu.VMEM((plane_count + 2, (local_rows + 2) * CH, cols), bf16),
        ],
        compiler_params=pltpu.CompilerParams(vmem_limit_bytes=16 * 2**20),
        name="score",
    )(packed, from_pair, from_other, project, first, second, consts)

    total = total[:4]
    summed = total + lax.ppermute(total, "disp", swap)
    coarse = summed[local_rows:] / summed[:local_rows]
    received = lax.ppermute(coarse, both, neighbours)
    far_rows = lax.ppermute(coarse, both, far)
    exchanged = lax.ppermute(received, "disp", swap)
    swapped = lax.ppermute(far_rows, "disp", swap)
    mix = pl.pallas_call(
        mixing_kernel,
        out_shape=jax.ShapeDtypeStruct((3 * local_rows, mask_weight.shape[1], cols), f32),
        in_specs=[vmem, vmem],
        out_specs=vmem,
        compiler_params=pltpu.CompilerParams(vmem_limit_bytes=4 * 2**20),
        name="mixing",
    )(left, mask_weight)
    refined = pl.pallas_call(
        functools.partial(refine_kernel, pix_size=pix_size),
        out_shape=jax.ShapeDtypeStruct((fine, width), f32),
        in_specs=[vmem] * 7,
        out_specs=vmem,
        compiler_params=pltpu.CompilerParams(vmem_limit_bytes=8 * 2**20),
        name="refine",
    )(coarse, received, exchanged, far_rows, swapped, mix, conf)
    return (coarse, refined)


def solution(mesh):
    rows = P(("grp", "pix"), None)
    placed = (rows, rows, P(), P(), P(), P(), P(), P(), P(), rows)
    return jax.shard_map(
        functools.partial(local, pix_size=mesh.shape["pix"], disp_size=mesh.shape["disp"]),
        mesh=mesh,
        in_specs=placed,
        out_specs=(rows, rows),
        check_vma=False,
    )
```

```python
import functools

import jax
import jax.numpy as jnp
from jax import lax
from jax.experimental import pallas as pl
from jax.experimental.pallas import tpu as pltpu
from jax.sharding import PartitionSpec as P

DSP = 128
UP = 4
TV_ITERS = 8
CH = 16

dual_step = 0.175
primal_step = 0.7
tv_bound = 0.3
cost_scale = 8.0
mask_scale = 3.0
f32 = jnp.float32
bf16 = jnp.bfloat16


def involution(pairs, pix_size, disp_size):
    perm = []
    used = set()
    for i, j in pairs:
        used |= {i, j}
        for d in range(disp_size):
            perm += [(i * disp_size + d, j * disp_size + d), (j * disp_size + d, i * disp_size + d)]
    for i in range(pix_size):
        if i not in used:
            perm += [(i * disp_size + d, i * disp_size + (d ^ 1)) for d in range(disp_size)]
    return sorted(perm)


def mixed_exchange(pix_size, disp_size):
    send = {}
    for i in range(pix_size):
        send[i, 0] = (i ^ 1, 0)
        j = i + 1 if i % 2 else i - 1
        send[i, 1] = (j, 1) if 0 <= j < pix_size else (i, 0)
    for end in (0, pix_size - 1):
        send[end ^ 1, 0] = (end, 1)
    order = sorted(send)
    return [tuple(p * disp_size + d for p, d in (key, send[key])) for key in order]


def sort_neighbours(received, swapped, pix, disp, pix_size):
    at_end = (pix == 0) | (pix == pix_size - 1)
    direct = (disp == 0) != at_end
    even = pix % 2 == 0
    first_is_below = direct == even
    below = jnp.where(first_is_below, received, swapped)
    above = jnp.where(first_is_below, swapped, received)
    return above, below


def split3(values):
    high = values.astype(bf16)
    rest = values - high.astype(f32)
    middle = rest.astype(bf16)
    low = (rest - middle.astype(f32)).astype(bf16)
    return high, middle, low


def phase_matrix(transposed):
    rows = lax.broadcasted_iota(jnp.int32, (256, 256), 0)
    cols = lax.broadcasted_iota(jnp.int32, (256, 256), 1)
    if transposed:
        rows, cols = cols, rows
    return jnp.where(rows == UP * (cols & 63) + (cols >> 6), 1.0, 0.0).astype(bf16)


def deinterleave(values):
    perm = phase_matrix(False)
    chunks = values.shape[1] // 256
    pieces = [
        jnp.dot(values[:, 256 * j : 256 * j + 256], perm, preferred_element_type=f32)
        for j in range(chunks)
    ]
    lane = lax.broadcasted_iota(jnp.int32, (values.shape[0], 128), 1)
    phases = []
    for b in range(UP):
        tiles = []
        for t in range(chunks // 2):
            first = pieces[2 * t][:, 128 * (b // 2) : 128 * (b // 2) + 128]
            second = pieces[2 * t + 1][:, 128 * (b // 2) : 128 * (b // 2) + 128]
            if b % 2 == 0:
                second = pltpu.roll(second, 64, 1)
            else:
                first = pltpu.roll(first, 64, 1)
            tiles.append(jnp.where(lane < 64, first, second))
        phases.append(jnp.concatenate(tiles, 1))
    return phases


def interleave(phases):
    rows = phases[0].shape[0]
    lane = lax.broadcasted_iota(jnp.int32, (rows, 128), 1)
    chunks = []
    for t in range(phases[0].shape[1] // 128):
        tiles = [phase[:, 128 * t : 128 * t + 128] for phase in phases]
        rolled = [pltpu.roll(tile, 64, 1) for tile in tiles]
        chunks.append([jnp.where(lane < 64, tiles[b], rolled[b + 1]) for b in (0, 2)])
        chunks.append([jnp.where(lane < 64, rolled[b], tiles[b + 1]) for b in (0, 2)])
    packed = jnp.concatenate([jnp.concatenate(chunk, 1) for chunk in chunks], 0)
    size = packed.shape[0]
    parts = jnp.concatenate(split3(packed), 0)
    moved = jnp.dot(parts, phase_matrix(True), preferred_element_type=f32)
    moved = (moved[2 * size :] + moved[size : 2 * size]) + moved[:size]
    return jnp.concatenate([moved[rows * j : rows * j + rows] for j in range(len(chunks))], 1)


def shift_right(values, amount=1):
    lane = lax.broadcasted_iota(jnp.int32, (values.shape[0], 128), 1)
    rolled = [pltpu.roll(values[:, t : t + 128], amount, 1) for t in range(0, values.shape[1], 128)]
    zero = jnp.zeros_like(rolled[0])
    return jnp.concatenate(
        [jnp.where(lane < amount, prev, now) for prev, now in zip([zero] + rolled[:-1], rolled)], 1
    )


def shift_left(values):
    lane = lax.broadcasted_iota(jnp.int32, (values.shape[0], 128), 1)
    rolled = [pltpu.roll(values[:, t : t + 128], 127, 1) for t in range(0, values.shape[1], 128)]
    zero = jnp.zeros_like(rolled[0])
    return jnp.concatenate(
        [jnp.where(lane == 127, after, now) for now, after in zip(rolled, rolled[1:] + [zero])], 1
    )


def join_taps(taps):
    size = taps.shape[0] // 3
    before = shift_right(taps[:size].astype(bf16)).astype(f32)
    after = shift_left(taps[2 * size :].astype(bf16)).astype(f32)
    return taps[size : 2 * size] + (before + after)


def score_kernel(
    own_ref,
    received_ref,
    exchanged_ref,
    project_ref,
    first_ref,
    second_ref,
    const_ref,
    total_ref,
    left_ref,
    conf_ref,
    volume,
    hidden,
    *,
    pix_size,
    disp_size,
):
    pix = lax.axis_index("pix")
    disp = lax.axis_index("disp")
    plane_count = DSP // disp_size
    even = pix % 2 == 0
    pair, other = (received_ref[...].astype(f32), exchanged_ref[...].astype(f32))
    above = jnp.where(even, other, pair)
    below = jnp.where(even, pair, other)
    gathered = jnp.concatenate([above, own_ref[...].astype(f32), below], 0).astype(bf16)
    phases = deinterleave(gathered)
    fine = own_ref.shape[0] // 3
    conf_ref[...] = jnp.concatenate(
        [
            jnp.concatenate([phase[s * 3 * fine + 2 * fine : s * 3 * fine + 3 * fine] for s in range(3)], 0)
            for phase in phases
        ],
        1,
    )
    stacked = jnp.concatenate(
        [
            phase[s * 3 * fine + img * fine : s * 3 * fine + (img + 1) * fine]
            for phase in phases
            for img in range(2)
            for s in range(3)
        ],
        0,
    )
    patches = (stacked / 64.0 - 2.0).astype(bf16)
    feats3 = jnp.dot(project_ref[...], patches, preferred_element_type=f32)
    size = feats3.shape[0] // 3
    feats = (feats3[2 * size :] + feats3[size : 2 * size]) + feats3[:size]
    half = size // 2
    rows = half // CH
    local_rows = rows // 3
    row_id = lax.broadcasted_iota(jnp.int32, (half, 1), 0) // CH + (pix - 1) * local_rows
    inside = (row_id >= 0) & (row_id < pix_size * local_rows)
    left = jnp.where(inside, feats[:half], 0.0).astype(bf16)
    right = feats[half:].astype(bf16).astype(f32)
    left_ref[...] = left
    lane = lax.broadcasted_iota(jnp.int32, right.shape, 1)
    start = disp * plane_count

    def shifted_by(amount):
        return jnp.where(lane >= amount, pltpu.roll(right, amount, 1), 0.0).astype(bf16)

    hid_rows, cols = hidden.shape[1:]
    windows = hid_rows // 32
    pair_count = plane_count // 2 + 1
    state = [shifted_by(start)]

    def fill(t):
        if t == 0:
            planes = [shifted_by(jnp.maximum(start - 2 + k, 0)) for k in range(2)]
            planes = [jnp.where(disp > 0, plane, jnp.zeros_like(plane)) for plane in planes]
        else:
            base = state[-1]
            step = 2 * ((t - 1) % 3)
            planes = [base if step + k == 0 else shift_right(base, step + k) for k in range(2)]
            if step == 4:
                state.append(shift_right(base, 6))
            if t == pair_count:
                exists = disp < disp_size - 1
                planes = [jnp.where(exists, plane, jnp.zeros_like(plane)) for plane in planes]
        for k in range(2):
            volume[2 * t + k] = left * planes[k]

    block_row = lax.broadcasted_iota(jnp.int32, (first_ref.shape[0], 1), 0) // CH
    live = [block_row >= 0 for _ in range(windows)]
    live[0] = (pix > 0) | ((block_row & 1) == 1)
    live[-1] = live[-1] & ((pix < pix_size - 1) | ((block_row & 1) == 0))
    first = [jnp.where(keep, first_ref[...].astype(f32), 0.0).astype(bf16) for keep in live]
    first_bias = [jnp.where(keep[:64], const_ref[0], 0.0) for keep in live]

    def conv_first(t):
        for window in range(windows):
            block = volume[2 * t : 2 * t + 4, 32 * window : 32 * window + 64, :]
            taps = jnp.dot(first[window], block.reshape(256, cols), preferred_element_type=f32)
            made = jnp.maximum(join_taps(taps) + first_bias[window], 0.0)
            halves = [made[:32], made[32:]]
            if t == 0:
                halves[0] = jnp.where(disp > 0, halves[0], 0.0)
            if t == pair_count - 1:
                halves[1] = jnp.where(disp < disp_size - 1, halves[1], 0.0)
            for k in range(2):
                hidden[2 * t + k, 32 * window : 32 * window + 32, :] = halves[k].astype(bf16)

    second = second_ref[...]
    second_bias = const_ref[1]
    head = const_ref[2]
    partial = []

    def conv_second(t):
        block = hidden[2 * t : 2 * t + 4]
        taps = jnp.dot(second, block.reshape(256, cols), preferred_element_type=f32)
        made = jnp.maximum(join_taps(taps) + second_bias, 0.0) * head
        partial.append(jnp.sum(made.reshape(8, 8, cols), 0))

    for t in range(pair_count + 1):
        fill(t)
    for t in range(pair_count):
        conv_first(t)
    for t in range(pair_count - 1):
        conv_second(t)

    row8 = lax.broadcasted_iota(jnp.int32, (8, cols), 0)
    weight = jnp.zeros((8, cols), f32)
    moment = jnp.zeros((8, cols), f32)
    upper = row8 < 4
    for t in range(0, plane_count // 2, 2):
        kept = jnp.where(upper, partial[t], partial[t + 1])
        other = jnp.where(upper, partial[t + 1], partial[t])
        raw = kept + pltpu.roll(other, 4, 0)
        expo = jnp.exp(-cost_scale * jnp.tanh(raw))
        plane = (start + 2 * t + (row8 >> 1)).astype(f32) / DSP
        weight = weight + expo
        moment = moment + expo * plane
    for turn in (4, 2):
        weight = weight + pltpu.roll(weight, turn, 0)
        moment = moment + pltpu.roll(moment, turn, 0)
    total_ref[...] = jnp.where((row8 & 3) < 2, weight, moment)


def mixing_kernel(left_ref, mask_weight_ref, mix_ref):
    cols = left_ref.shape[1]
    kinds = mask_weight_ref.shape[1]
    new = lax.broadcasted_iota(jnp.int32, (kinds, kinds), 0)
    old = lax.broadcasted_iota(jnp.int32, (kinds, kinds), 1)
    swapped = (new & ~15) + (new & 3) * UP + ((new >> 2) & 3)
    swapped = jnp.where(old == swapped, 1.0, 0.0).astype(bf16)
    mask = jnp.concatenate(
        [
            lax.dot_general(
                swapped, part, (((1,), (1,)), ((), ())), preferred_element_type=f32
            ).astype(bf16)
            for part in split3(mask_weight_ref[...])
        ],
        0,
    )
    for r in range(mix_ref.shape[0]):
        logits3 = jnp.dot(mask, left_ref[CH * r : CH * r + CH, :], preferred_element_type=f32)
        logits = (logits3[2 * kinds :] + logits3[kinds : 2 * kinds]) + logits3[:kinds]
        expo = jnp.exp(mask_scale * jnp.tanh(logits)).reshape(9, UP * UP, cols)
        mix_ref[r] = (expo / jnp.sum(expo, 0)).reshape(kinds, cols)


def refine_kernel(
    own_ref,
    received_ref,
    exchanged_ref,
    far_ref,
    swapped_ref,
    mix_ref,
    conf_ref,
    out_ref,
    *,
    pix_size,
):
    pix = lax.axis_index("pix")
    disp = lax.axis_index("disp")
    local = own_ref.shape[0]
    above, below = sort_neighbours(received_ref[...], exchanged_ref[...], pix, disp, pix_size)
    first_core = disp == 0
    far_below = jnp.where(first_core, far_ref[...], swapped_ref[...])
    far_above = jnp.where(first_core, swapped_ref[...], far_ref[...])
    window = [far_above[local - 1 :], above, own_ref[...], below, far_below[:1]]
    window = jnp.concatenate(window, 0)
    cols = window.shape[1]
    row_id = lax.broadcasted_iota(jnp.int32, window.shape, 0) + pix * local - local - 1
    window = jnp.where((row_id >= 0) & (row_id < pix_size * local), window, 0.0)
    moved = [shift_right(window), window, shift_left(window)]
    phases = [[] for _ in range(UP)]
    for r in range(3 * local):
        mixing = mix_ref[r]
        total = jnp.zeros((UP * UP, cols), f32)
        for k in range(9):
            near = moved[k % 3][r + k // 3 : r + k // 3 + 1]
            total = total + mixing[UP * UP * k : UP * UP * k + UP * UP] * near
        for b in range(UP):
            phases[b].append(total[UP * b : UP * b + UP])
    target = jnp.concatenate([jnp.concatenate(phase, 0) for phase in phases], 1)
    fine = target.shape[0]
    out_rows = fine // 3
    conf = conf_ref[...]
    lanes = target.shape[1]
    global_row = lax.broadcasted_iota(jnp.int32, target.shape, 0) + (pix - 1) * out_rows
    row_inside = (global_row >= 0) & (global_row < pix_size * out_rows - 1)
    target = target * (dual_step / tv_bound)
    anchor = primal_step * conf * target
    scale = 1.0 / (1.0 + primal_step * conf)
    keep_y = jnp.where(row_inside, 1.0, 0.0)
    last_lane = lax.broadcasted_iota(jnp.int32, (fine, cols), 1) == cols - 1
    primal = target
    extrap = target
    dual_x = None
    for _ in range(TV_ITERS):
        trial_y = keep_y * (pltpu.roll(extrap, fine - 1, 0) - extrap)
        wrapped = jnp.where(last_lane, extrap[:, lanes - cols :], shift_left(extrap[:, :cols]))
        trial_x = jnp.concatenate([extrap[:, cols:], wrapped], 1) - extrap
        if dual_x is not None:
            trial_x = dual_x + trial_x
            trial_y = dual_y + trial_y
        shrink = lax.rsqrt(jnp.maximum(1.0, trial_x * trial_x + trial_y * trial_y))
        dual_x = trial_x * shrink
        dual_y = trial_y * shrink
        upper = pltpu.roll(dual_y, 1, 0)
        behind = jnp.concatenate([shift_right(dual_x[:, lanes - cols :]), dual_x[:, : lanes - cols]], 1)
        divergence = dual_x - behind + dual_y - upper
        updated = (primal + (primal_step * dual_step) * divergence + anchor) * scale
        extrap = 2.0 * updated - primal
        primal = updated
    primal = primal * (tv_bound / dual_step)
    kept = primal[out_rows : 2 * out_rows]
    out_ref[...] = interleave([kept[:, b * cols : (b + 1) * cols] for b in range(UP)])


def in_hbm(values):
    return pltpu.with_memory_space_constraint(values, pltpu.HBM)


def pack_kernel(left_ref, right_ref, conf_ref, out_ref, images, conf, sems):
    copies = [
        pltpu.make_async_copy(left_ref, images.at[0], sems.at[0]),
        pltpu.make_async_copy(right_ref, images.at[1], sems.at[1]),
        pltpu.make_async_copy(conf_ref, conf, sems.at[2]),
    ]
    for copy in copies:
        copy.start()
    for copy in copies:
        copy.wait()
    parts = [images[0].astype(f32), images[1].astype(f32), conf[...]]
    out_ref[...] = jnp.concatenate(parts, 0).astype(bf16)


def transposed(values):
    size = values.shape[1]
    eye = lax.broadcasted_iota(jnp.int32, (size, size), 0) == lax.broadcasted_iota(
        jnp.int32, (size, size), 1
    )
    eye = jnp.where(eye, 1.0, 0.0).astype(bf16)
    flipped = lax.dot_general(
        eye, values, (((1,), (1,)), ((), ())), preferred_element_type=f32
    )
    return flipped.astype(bf16)


def column(values, index):
    count = values.shape[0]
    lane = lax.broadcasted_iota(jnp.int32, (index.shape[0], count), 1)
    wide = jnp.broadcast_to(values.reshape(1, count), (index.shape[0], count))
    return jnp.sum(jnp.where(lane == index, wide, 0.0), 1, keepdims=True)


def prepare_kernel(
    feat_ref,
    first_weight_ref,
    first_bias_ref,
    second_weight_ref,
    second_bias_ref,
    head_ref,
    project_ref,
    first_ref,
    second_ref,
    const_ref,
    weights,
    sems,
):
    copies = [
        pltpu.make_async_copy(ref, weights.at[n], sems.at[n])
        for n, ref in enumerate((first_weight_ref, second_weight_ref))
    ]
    for copy in copies:
        copy.start()

    size = project_ref.shape[1]
    groups = size // (UP * UP)
    pixel = lax.broadcasted_iota(jnp.int32, (UP * UP, size), 0)
    spot = lax.broadcasted_iota(jnp.int32, (UP * UP, size), 1)
    expand = jnp.where(pixel == UP * (spot % UP) + spot // (UP * groups), 1.0, 0.0).astype(bf16)
    own_group = lax.broadcasted_iota(jnp.int32, (size, size), 0) // CH
    keep = own_group == (lax.broadcasted_iota(jnp.int32, (size, size), 1) // UP) % groups
    for n, part in enumerate(split3(feat_ref[...])):
        wide = jnp.dot(transposed(part), expand, preferred_element_type=f32)
        wide = jnp.concatenate([wide] * groups, 0)
        project_ref[size * n : size * n + size, :] = jnp.where(keep, wide, 0.0).astype(bf16)

    index = lax.broadcasted_iota(jnp.int32, (64, 1), 0)
    shape = const_ref.shape[1:]
    const_ref[0] = jnp.broadcast_to(column(first_bias_ref[...], index % CH), shape)
    const_ref[1] = jnp.broadcast_to(column(second_bias_ref[...], index // 4), shape)
    const_ref[2] = jnp.broadcast_to(column(head_ref[...], index // 4), shape)

    for copy in copies:
        copy.wait()
    taps = weights.shape[1] ** 3 * CH
    flat = [transposed(weights[n].reshape(taps, CH)) for n in range(2)]
    flat = jnp.concatenate(flat, 0)
    source = lax.broadcasted_iota(jnp.int32, (taps, 256), 0)
    lane = lax.broadcasted_iota(jnp.int32, (1, 256), 1)
    plane, row, chan = (lane >> 6, (lane >> 4) & 3, lane & 15)
    out_row = lax.broadcasted_iota(jnp.int32, (64, 64), 0)
    out_col = lax.broadcasted_iota(jnp.int32, (64, 64), 1)
    regroup = jnp.where(out_col == (out_row & 3) * CH + (out_row >> 2), 1.0, 0.0).astype(bf16)
    for tap in range(3):
        wanted = jnp.where((plane < 3) & (row < 3), ((plane * 3 + row) * 3 + tap) * CH + chan, -1)
        select = jnp.where(source == wanted, 1.0, 0.0).astype(bf16)
        base = jnp.dot(flat, select, preferred_element_type=f32)
        placed = [base] + [pltpu.roll(base, 64 * (j // 2) + CH * (j % 2), 1) for j in range(1, 4)]
        blocks = [jnp.concatenate([p[n * CH : n * CH + CH] for p in placed], 0) for n in range(2)]
        first_ref[64 * tap : 64 * tap + 64, :] = blocks[0].astype(bf16)
        mixed = jnp.dot(regroup, blocks[1].astype(bf16), preferred_element_type=f32)
        second_ref[64 * tap : 64 * tap + 64, :] = mixed.astype(bf16)


def local(
    left_image,
    right_image,
    feat_weight,
    first_weight,
    first_bias,
    second_weight,
    second_bias,
    head_weight,
    mask_weight,
    confidence,
    *,
    pix_size,
    disp_size,
):
    both = ("pix", "disp")
    fine, width = left_image.shape
    cols = width // UP
    local_rows = fine // UP
    plane_count = DSP // disp_size
    swap = [(d, d ^ 1) for d in range(disp_size)]
    neighbours = mixed_exchange(pix_size, disp_size)
    pairs = involution([(i, i + 1) for i in range(0, pix_size - 1, 2)], pix_size, disp_size)
    others = involution([(i, i + 1) for i in range(1, pix_size - 1, 2)], pix_size, disp_size)
    far = []
    taken = set()
    for i in range(pix_size - 2):
        a, b = (i * disp_size, (i + 2) * disp_size + 1)
        far += [(a, b), (b, a)]
        taken |= {a, b}
    spare = [n for n in range(pix_size * disp_size) if n not in taken]
    for a, b in zip(spare[::2], spare[1::2]):
        far += [(a, b), (b, a)]
    far = sorted(far)

    vmem = pl.BlockSpec(memory_space=pltpu.VMEM)
    hbm = pl.BlockSpec(memory_space=pltpu.HBM)
    packed = pl.pallas_call(
        pack_kernel,
        out_shape=jax.ShapeDtypeStruct((3 * fine, width), bf16),
        in_specs=[hbm] * 3,
        out_specs=vmem,
        scratch_shapes=[
            pltpu.VMEM((2, fine, width), left_image.dtype),
            pltpu.VMEM((fine, width), f32),
            pltpu.SemaphoreType.DMA((3,)),
        ],
        compiler_params=pltpu.CompilerParams(vmem_limit_bytes=2 * 2**20),
        name="pack",
    )(in_hbm(left_image), in_hbm(right_image), in_hbm(confidence))
    from_pair = lax.ppermute(packed, both, pairs)
    from_other = lax.ppermute(packed, both, others)

    groups = 6 * local_rows
    project, first, second, consts = pl.pallas_call(
        prepare_kernel,
        out_shape=(
            jax.ShapeDtypeStruct((3 * groups * CH, groups * UP * UP), bf16),
            jax.ShapeDtypeStruct((192, 256), bf16),
            jax.ShapeDtypeStruct((192, 256), bf16),
            jax.ShapeDtypeStruct((3, 64, cols), f32),
        ),
        in_specs=[vmem, hbm, vmem, hbm, vmem, vmem],
        out_specs=(vmem,) * 4,
        scratch_shapes=[
            pltpu.VMEM((2,) + first_weight.shape, bf16),
            pltpu.SemaphoreType.DMA((2,)),
        ],
        compiler_params=pltpu.CompilerParams(vmem_limit_bytes=8 * 2**20),
        name="prepare",
    )(
        feat_weight,
        in_hbm(first_weight),
        first_bias,
        in_hbm(second_weight),
        second_bias,
        head_weight,
    )
    total, left, conf = pl.pallas_call(
        functools.partial(score_kernel, pix_size=pix_size, disp_size=disp_size),
        out_shape=(
            jax.ShapeDtypeStruct((8, cols), f32),
            jax.ShapeDtypeStruct((3 * local_rows * CH, cols), bf16),
            jax.ShapeDtypeStruct((3 * fine, width), f32),
        ),
        in_specs=[vmem] * 7,
        out_specs=(vmem, vmem, vmem),
        scratch_shapes=[
            pltpu.VMEM((plane_count + 4, 3 * local_rows * CH, cols), bf16),
            pltpu.VMEM((plane_count + 2, (local_rows + 2) * CH, cols), bf16),
        ],
        compiler_params=pltpu.CompilerParams(vmem_limit_bytes=16 * 2**20),
        name="score",
    )(packed, from_pair, from_other, project, first, second, consts)

    total = total[:4]
    summed = total + lax.ppermute(total, "disp", swap)
    coarse = summed[local_rows:] / summed[:local_rows]
    received = lax.ppermute(coarse, both, neighbours)
    far_rows = lax.ppermute(coarse, both, far)
    exchanged = lax.ppermute(received, "disp", swap)
    swapped = lax.ppermute(far_rows, "disp", swap)
    mix = pl.pallas_call(
        mixing_kernel,
        out_shape=jax.ShapeDtypeStruct((3 * local_rows, mask_weight.shape[1], cols), f32),
        in_specs=[vmem, vmem],
        out_specs=vmem,
        compiler_params=pltpu.CompilerParams(vmem_limit_bytes=4 * 2**20),
        name="mixing",
    )(left, mask_weight)
    refined = pl.pallas_call(
        functools.partial(refine_kernel, pix_size=pix_size),
        out_shape=jax.ShapeDtypeStruct((fine, width), f32),
        in_specs=[vmem] * 7,
        out_specs=vmem,
        compiler_params=pltpu.CompilerParams(vmem_limit_bytes=8 * 2**20),
        name="refine",
    )(coarse, received, exchanged, far_rows, swapped, mix, conf)
    return (coarse, refined)


def solution(mesh):
    rows = P(("grp", "pix"), None)
    placed = (rows, rows, P(), P(), P(), P(), P(), P(), P(), rows)
    return jax.shard_map(
        functools.partial(local, pix_size=mesh.shape["pix"], disp_size=mesh.shape["disp"]),
        mesh=mesh,
        in_specs=placed,
        out_specs=(rows, rows),
        check_vma=False,
    )
```

```python
import functools

import jax
import jax.numpy as jnp
from jax import lax
from jax.experimental import pallas as pl
from jax.experimental.pallas import tpu as pltpu
from jax.sharding import PartitionSpec as P

DSP = 128
UP = 4
TV_ITERS = 8
CH = 16

dual_step = 0.175
primal_step = 0.7
tv_bound = 0.3
cost_scale = 8.0
mask_scale = 3.0
f32 = jnp.float32
bf16 = jnp.bfloat16


def involution(pairs, pix_size, disp_size):
    perm = []
    used = set()
    for i, j in pairs:
        used |= {i, j}
        for d in range(disp_size):
            perm += [(i * disp_size + d, j * disp_size + d), (j * disp_size + d, i * disp_size + d)]
    for i in range(pix_size):
        if i not in used:
            perm += [(i * disp_size + d, i * disp_size + (d ^ 1)) for d in range(disp_size)]
    return sorted(perm)


def mixed_exchange(pix_size, disp_size):
    send = {}
    for i in range(pix_size):
        send[i, 0] = (i ^ 1, 0)
        j = i + 1 if i % 2 else i - 1
        send[i, 1] = (j, 1) if 0 <= j < pix_size else (i, 0)
    for end in (0, pix_size - 1):
        send[end ^ 1, 0] = (end, 1)
    order = sorted(send)
    return [tuple(p * disp_size + d for p, d in (key, send[key])) for key in order]


def sort_neighbours(received, swapped, pix, disp, pix_size):
    at_end = (pix == 0) | (pix == pix_size - 1)
    direct = (disp == 0) != at_end
    even = pix % 2 == 0
    first_is_below = direct == even
    below = jnp.where(first_is_below, received, swapped)
    above = jnp.where(first_is_below, swapped, received)
    return above, below


def split3(values):
    high = values.astype(bf16)
    rest = values - high.astype(f32)
    middle = rest.astype(bf16)
    low = (rest - middle.astype(f32)).astype(bf16)
    return high, middle, low


def phase_matrix(transposed):
    rows = lax.broadcasted_iota(jnp.int32, (256, 256), 0)
    cols = lax.broadcasted_iota(jnp.int32, (256, 256), 1)
    if transposed:
        rows, cols = cols, rows
    return jnp.where(rows == UP * (cols & 63) + (cols >> 6), 1.0, 0.0).astype(bf16)


def deinterleave(values):
    perm = phase_matrix(False)
    chunks = values.shape[1] // 256
    pieces = [
        jnp.dot(values[:, 256 * j : 256 * j + 256], perm, preferred_element_type=f32)
        for j in range(chunks)
    ]
    lane = lax.broadcasted_iota(jnp.int32, (values.shape[0], 128), 1)
    phases = []
    for b in range(UP):
        tiles = []
        for t in range(chunks // 2):
            first = pieces[2 * t][:, 128 * (b // 2) : 128 * (b // 2) + 128]
            second = pieces[2 * t + 1][:, 128 * (b // 2) : 128 * (b // 2) + 128]
            if b % 2 == 0:
                second = pltpu.roll(second, 64, 1)
            else:
                first = pltpu.roll(first, 64, 1)
            tiles.append(jnp.where(lane < 64, first, second))
        phases.append(jnp.concatenate(tiles, 1))
    return phases


def interleave(phases):
    rows = phases[0].shape[0]
    lane = lax.broadcasted_iota(jnp.int32, (rows, 128), 1)
    chunks = []
    for t in range(phases[0].shape[1] // 128):
        tiles = [phase[:, 128 * t : 128 * t + 128] for phase in phases]
        rolled = [pltpu.roll(tile, 64, 1) for tile in tiles]
        chunks.append([jnp.where(lane < 64, tiles[b], rolled[b + 1]) for b in (0, 2)])
        chunks.append([jnp.where(lane < 64, rolled[b], tiles[b + 1]) for b in (0, 2)])
    packed = jnp.concatenate([jnp.concatenate(chunk, 1) for chunk in chunks], 0)
    size = packed.shape[0]
    parts = jnp.concatenate(split3(packed), 0)
    moved = jnp.dot(parts, phase_matrix(True), preferred_element_type=f32)
    moved = (moved[2 * size :] + moved[size : 2 * size]) + moved[:size]
    return jnp.concatenate([moved[rows * j : rows * j + rows] for j in range(len(chunks))], 1)


def shift_right(values, amount=1):
    lane = lax.broadcasted_iota(jnp.int32, (values.shape[0], 128), 1)
    rolled = [pltpu.roll(values[:, t : t + 128], amount, 1) for t in range(0, values.shape[1], 128)]
    zero = jnp.zeros_like(rolled[0])
    return jnp.concatenate(
        [jnp.where(lane < amount, prev, now) for prev, now in zip([zero] + rolled[:-1], rolled)], 1
    )


def shift_left(values):
    lane = lax.broadcasted_iota(jnp.int32, (values.shape[0], 128), 1)
    rolled = [pltpu.roll(values[:, t : t + 128], 127, 1) for t in range(0, values.shape[1], 128)]
    zero = jnp.zeros_like(rolled[0])
    return jnp.concatenate(
        [jnp.where(lane == 127, after, now) for now, after in zip(rolled, rolled[1:] + [zero])], 1
    )


def join_taps(taps):
    size = taps.shape[0] // 3
    before = shift_right(taps[:size].astype(bf16)).astype(f32)
    after = shift_left(taps[2 * size :].astype(bf16)).astype(f32)
    return taps[size : 2 * size] + (before + after)


def score_kernel(
    own_ref,
    received_ref,
    exchanged_ref,
    project_ref,
    first_ref,
    second_ref,
    const_ref,
    total_ref,
    left_ref,
    conf_ref,
    volume,
    hidden,
    *,
    pix_size,
    disp_size,
):
    pix = lax.axis_index("pix")
    disp = lax.axis_index("disp")
    plane_count = DSP // disp_size
    even = pix % 2 == 0
    pair, other = (received_ref[...].astype(f32), exchanged_ref[...].astype(f32))
    above = jnp.where(even, other, pair)
    below = jnp.where(even, pair, other)
    gathered = jnp.concatenate([above, own_ref[...].astype(f32), below], 0).astype(bf16)
    phases = deinterleave(gathered)
    fine = own_ref.shape[0] // 3
    conf_ref[...] = jnp.concatenate(
        [
            jnp.concatenate([phase[s * 3 * fine + 2 * fine : s * 3 * fine + 3 * fine] for s in range(3)], 0)
            for phase in phases
        ],
        1,
    )
    stacked = jnp.concatenate(
        [
            phase[s * 3 * fine + img * fine : s * 3 * fine + (img + 1) * fine]
            for phase in phases
            for img in range(2)
            for s in range(3)
        ],
        0,
    )
    patches = (stacked / 64.0 - 2.0).astype(bf16)
    feats3 = jnp.dot(project_ref[...], patches, preferred_element_type=f32)
    size = feats3.shape[0] // 3
    feats = (feats3[2 * size :] + feats3[size : 2 * size]) + feats3[:size]
    half = size // 2
    rows = half // CH
    local_rows = rows // 3
    row_id = lax.broadcasted_iota(jnp.int32, (half, 1), 0) // CH + (pix - 1) * local_rows
    inside = (row_id >= 0) & (row_id < pix_size * local_rows)
    left = jnp.where(inside, feats[:half], 0.0).astype(bf16)
    right = feats[half:].astype(bf16).astype(f32)
    left_ref[...] = left
    lane = lax.broadcasted_iota(jnp.int32, right.shape, 1)
    start = disp * plane_count

    def shifted_by(amount):
        return jnp.where(lane >= amount, pltpu.roll(right, amount, 1), 0.0).astype(bf16)

    hid_rows, cols = hidden.shape[1:]
    windows = hid_rows // 32
    pair_count = plane_count // 2 + 1
    state = [shifted_by(start)]

    def fill(t):
        if t == 0:
            planes = [shifted_by(jnp.maximum(start - 2 + k, 0)) for k in range(2)]
            planes = [jnp.where(disp > 0, plane, jnp.zeros_like(plane)) for plane in planes]
        else:
            base = state[-1]
            step = 2 * ((t - 1) % 3)
            planes = [base if step + k == 0 else shift_right(base, step + k) for k in range(2)]
            if step == 4:
                state.append(shift_right(base, 6))
            if t == pair_count:
                exists = disp < disp_size - 1
                planes = [jnp.where(exists, plane, jnp.zeros_like(plane)) for plane in planes]
        for k in range(2):
            volume[2 * t + k] = left * planes[k]

    block_row = lax.broadcasted_iota(jnp.int32, (first_ref.shape[0], 1), 0) // CH
    live = [block_row >= 0 for _ in range(windows)]
    live[0] = (pix > 0) | ((block_row & 1) == 1)
    live[-1] = live[-1] & ((pix < pix_size - 1) | ((block_row & 1) == 0))
    first = [jnp.where(keep, first_ref[...].astype(f32), 0.0).astype(bf16) for keep in live]
    first_bias = [jnp.where(keep[:64], const_ref[0], 0.0) for keep in live]

    def conv_first(t):
        for window in range(windows):
            block = volume[2 * t : 2 * t + 4, 32 * window : 32 * window + 64, :]
            taps = jnp.dot(first[window], block.reshape(256, cols), preferred_element_type=f32)
            made = jnp.maximum(join_taps(taps) + first_bias[window], 0.0)
            halves = [made[:32], made[32:]]
            if t == 0:
                halves[0] = jnp.where(disp > 0, halves[0], 0.0)
            if t == pair_count - 1:
                halves[1] = jnp.where(disp < disp_size - 1, halves[1], 0.0)
            for k in range(2):
                hidden[2 * t + k, 32 * window : 32 * window + 32, :] = halves[k].astype(bf16)

    second = second_ref[...]
    second_bias = const_ref[1]
    head = const_ref[2]
    partial = []

    def conv_second(t):
        block = hidden[2 * t : 2 * t + 4]
        taps = jnp.dot(second, block.reshape(256, cols), preferred_element_type=f32)
        made = jnp.maximum(join_taps(taps) + second_bias, 0.0) * head
        partial.append(jnp.sum(made.reshape(8, 8, cols), 0))

    for t in range(pair_count + 1):
        fill(t)
    for t in range(pair_count):
        conv_first(t)
    for t in range(pair_count - 1):
        conv_second(t)

    row8 = lax.broadcasted_iota(jnp.int32, (8, cols), 0)
    weight = jnp.zeros((8, cols), f32)
    moment = jnp.zeros((8, cols), f32)
    upper = row8 < 4
    for t in range(0, plane_count // 2, 2):
        kept = jnp.where(upper, partial[t], partial[t + 1])
        other = jnp.where(upper, partial[t + 1], partial[t])
        raw = kept + pltpu.roll(other, 4, 0)
        expo = jnp.exp(-cost_scale * jnp.tanh(raw))
        plane = (start + 2 * t + (row8 >> 1)).astype(f32) / DSP
        weight = weight + expo
        moment = moment + expo * plane
    for turn in (4, 2):
        weight = weight + pltpu.roll(weight, turn, 0)
        moment = moment + pltpu.roll(moment, turn, 0)
    total_ref[...] = jnp.where((row8 & 3) < 2, weight, moment)


def mixing_kernel(left_ref, mask_weight_ref, mix_ref):
    cols = left_ref.shape[1]
    kinds = mask_weight_ref.shape[1]
    new = lax.broadcasted_iota(jnp.int32, (kinds, kinds), 0)
    old = lax.broadcasted_iota(jnp.int32, (kinds, kinds), 1)
    swapped = (new & ~15) + (new & 3) * UP + ((new >> 2) & 3)
    swapped = jnp.where(old == swapped, 1.0, 0.0).astype(bf16)
    mask = jnp.concatenate(
        [
            lax.dot_general(
                swapped, part, (((1,), (1,)), ((), ())), preferred_element_type=f32
            ).astype(bf16)
            for part in split3(mask_weight_ref[...])
        ],
        0,
    )
    for r in range(mix_ref.shape[0]):
        logits3 = jnp.dot(mask, left_ref[CH * r : CH * r + CH, :], preferred_element_type=f32)
        logits = (logits3[2 * kinds :] + logits3[kinds : 2 * kinds]) + logits3[:kinds]
        expo = jnp.exp(mask_scale * jnp.tanh(logits)).reshape(9, UP * UP, cols)
        mix_ref[r] = (expo / jnp.sum(expo, 0)).reshape(kinds, cols)


def refine_kernel(
    own_ref,
    received_ref,
    exchanged_ref,
    far_ref,
    swapped_ref,
    mix_ref,
    conf_ref,
    out_ref,
    *,
    pix_size,
):
    pix = lax.axis_index("pix")
    disp = lax.axis_index("disp")
    local = own_ref.shape[0]
    above, below = sort_neighbours(received_ref[...], exchanged_ref[...], pix, disp, pix_size)
    first_core = disp == 0
    far_below = jnp.where(first_core, far_ref[...], swapped_ref[...])
    far_above = jnp.where(first_core, swapped_ref[...], far_ref[...])
    window = [far_above[local - 1 :], above, own_ref[...], below, far_below[:1]]
    window = jnp.concatenate(window, 0)
    cols = window.shape[1]
    row_id = lax.broadcasted_iota(jnp.int32, window.shape, 0) + pix * local - local - 1
    window = jnp.where((row_id >= 0) & (row_id < pix_size * local), window, 0.0)
    moved = [shift_right(window), window, shift_left(window)]
    phases = [[] for _ in range(UP)]
    for r in range(3 * local):
        mixing = mix_ref[r]
        total = jnp.zeros((UP * UP, cols), f32)
        for k in range(9):
            near = moved[k % 3][r + k // 3 : r + k // 3 + 1]
            total = total + mixing[UP * UP * k : UP * UP * k + UP * UP] * near
        for b in range(UP):
            phases[b].append(total[UP * b : UP * b + UP])
    target = jnp.concatenate([jnp.concatenate(phase, 0) for phase in phases], 1)
    fine = target.shape[0]
    out_rows = fine // 3
    conf = conf_ref[...]
    lanes = target.shape[1]
    global_row = lax.broadcasted_iota(jnp.int32, target.shape, 0) + (pix - 1) * out_rows
    row_inside = (global_row >= 0) & (global_row < pix_size * out_rows - 1)
    target = target * (dual_step / tv_bound)
    anchor = primal_step * conf * target
    scale = 1.0 / (1.0 + primal_step * conf)
    keep_y = jnp.where(row_inside, 1.0, 0.0)
    last_lane = lax.broadcasted_iota(jnp.int32, (fine, cols), 1) == cols - 1
    primal = target
    extrap = target
    dual_x = None
    for _ in range(TV_ITERS):
        trial_y = keep_y * (pltpu.roll(extrap, fine - 1, 0) - extrap)
        wrapped = jnp.where(last_lane, extrap[:, lanes - cols :], shift_left(extrap[:, :cols]))
        trial_x = jnp.concatenate([extrap[:, cols:], wrapped], 1) - extrap
        if dual_x is not None:
            trial_x = dual_x + trial_x
            trial_y = dual_y + trial_y
        shrink = lax.rsqrt(jnp.maximum(1.0, trial_x * trial_x + trial_y * trial_y))
        dual_x = trial_x * shrink
        dual_y = trial_y * shrink
        upper = pltpu.roll(dual_y, 1, 0)
        behind = jnp.concatenate([shift_right(dual_x[:, lanes - cols :]), dual_x[:, : lanes - cols]], 1)
        divergence = dual_x - behind + dual_y - upper
        updated = (primal + (primal_step * dual_step) * divergence + anchor) * scale
        extrap = 2.0 * updated - primal
        primal = updated
    primal = primal * (tv_bound / dual_step)
    kept = primal[out_rows : 2 * out_rows]
    out_ref[...] = interleave([kept[:, b * cols : (b + 1) * cols] for b in range(UP)])


def in_hbm(values):
    return pltpu.with_memory_space_constraint(values, pltpu.HBM)


def pack_kernel(left_ref, right_ref, conf_ref, out_ref, images, conf, sems):
    copies = [
        pltpu.make_async_copy(left_ref, images.at[0], sems.at[0]),
        pltpu.make_async_copy(right_ref, images.at[1], sems.at[1]),
        pltpu.make_async_copy(conf_ref, conf, sems.at[2]),
    ]
    for copy in copies:
        copy.start()
    for copy in copies:
        copy.wait()
    parts = [images[0].astype(f32), images[1].astype(f32), conf[...]]
    out_ref[...] = jnp.concatenate(parts, 0).astype(bf16)


def transposed(values):
    size = values.shape[1]
    eye = lax.broadcasted_iota(jnp.int32, (size, size), 0) == lax.broadcasted_iota(
        jnp.int32, (size, size), 1
    )
    eye = jnp.where(eye, 1.0, 0.0).astype(bf16)
    flipped = lax.dot_general(
        eye, values, (((1,), (1,)), ((), ())), preferred_element_type=f32
    )
    return flipped.astype(bf16)


def column(values, index):
    count = values.shape[0]
    lane = lax.broadcasted_iota(jnp.int32, (index.shape[0], count), 1)
    wide = jnp.broadcast_to(values.reshape(1, count), (index.shape[0], count))
    return jnp.sum(jnp.where(lane == index, wide, 0.0), 1, keepdims=True)


def prepare_kernel(
    feat_ref,
    first_weight_ref,
    first_bias_ref,
    second_weight_ref,
    second_bias_ref,
    head_ref,
    project_ref,
    first_ref,
    second_ref,
    const_ref,
    weights,
    sems,
):
    copies = [
        pltpu.make_async_copy(ref, weights.at[n], sems.at[n])
        for n, ref in enumerate((second_weight_ref,))
    ]
    for copy in copies:
        copy.start()

    size = project_ref.shape[1]
    groups = size // (UP * UP)
    pixel = lax.broadcasted_iota(jnp.int32, (UP * UP, size), 0)
    spot = lax.broadcasted_iota(jnp.int32, (UP * UP, size), 1)
    expand = jnp.where(pixel == UP * (spot % UP) + spot // (UP * groups), 1.0, 0.0).astype(bf16)
    own_group = lax.broadcasted_iota(jnp.int32, (size, size), 0) // CH
    keep = own_group == (lax.broadcasted_iota(jnp.int32, (size, size), 1) // UP) % groups
    for n, part in enumerate(split3(feat_ref[...])):
        wide = jnp.dot(transposed(part), expand, preferred_element_type=f32)
        wide = jnp.concatenate([wide] * groups, 0)
        project_ref[size * n : size * n + size, :] = jnp.where(keep, wide, 0.0).astype(bf16)

    index = lax.broadcasted_iota(jnp.int32, (64, 1), 0)
    shape = const_ref.shape[1:]
    const_ref[0] = jnp.broadcast_to(column(first_bias_ref[...], index % CH), shape)
    const_ref[1] = jnp.broadcast_to(column(second_bias_ref[...], index // 4), shape)
    const_ref[2] = jnp.broadcast_to(column(head_ref[...], index // 4), shape)

    taps = weights.shape[1] ** 3 * CH
    flat = [transposed(first_weight_ref[...].reshape(taps, CH))]
    copies[0].wait()
    flat.append(transposed(weights[0].reshape(taps, CH)))
    flat = jnp.concatenate(flat, 0)
    source = lax.broadcasted_iota(jnp.int32, (taps, 256), 0)
    lane = lax.broadcasted_iota(jnp.int32, (1, 256), 1)
    plane, row, chan = (lane >> 6, (lane >> 4) & 3, lane & 15)
    out_row = lax.broadcasted_iota(jnp.int32, (64, 64), 0)
    out_col = lax.broadcasted_iota(jnp.int32, (64, 64), 1)
    regroup = jnp.where(out_col == (out_row & 3) * CH + (out_row >> 2), 1.0, 0.0).astype(bf16)
    for tap in range(3):
        wanted = jnp.where((plane < 3) & (row < 3), ((plane * 3 + row) * 3 + tap) * CH + chan, -1)
        select = jnp.where(source == wanted, 1.0, 0.0).astype(bf16)
        base = jnp.dot(flat, select, preferred_element_type=f32)
        placed = [base] + [pltpu.roll(base, 64 * (j // 2) + CH * (j % 2), 1) for j in range(1, 4)]
        blocks = [jnp.concatenate([p[n * CH : n * CH + CH] for p in placed], 0) for n in range(2)]
        first_ref[64 * tap : 64 * tap + 64, :] = blocks[0].astype(bf16)
        mixed = jnp.dot(regroup, blocks[1].astype(bf16), preferred_element_type=f32)
        second_ref[64 * tap : 64 * tap + 64, :] = mixed.astype(bf16)


def local(
    left_image,
    right_image,
    feat_weight,
    first_weight,
    first_bias,
    second_weight,
    second_bias,
    head_weight,
    mask_weight,
    confidence,
    *,
    pix_size,
    disp_size,
):
    both = ("pix", "disp")
    fine, width = left_image.shape
    cols = width // UP
    local_rows = fine // UP
    plane_count = DSP // disp_size
    swap = [(d, d ^ 1) for d in range(disp_size)]
    neighbours = mixed_exchange(pix_size, disp_size)
    pairs = involution([(i, i + 1) for i in range(0, pix_size - 1, 2)], pix_size, disp_size)
    others = involution([(i, i + 1) for i in range(1, pix_size - 1, 2)], pix_size, disp_size)
    far = []
    taken = set()
    for i in range(pix_size - 2):
        a, b = (i * disp_size, (i + 2) * disp_size + 1)
        far += [(a, b), (b, a)]
        taken |= {a, b}
    spare = [n for n in range(pix_size * disp_size) if n not in taken]
    for a, b in zip(spare[::2], spare[1::2]):
        far += [(a, b), (b, a)]
    far = sorted(far)

    vmem = pl.BlockSpec(memory_space=pltpu.VMEM)
    hbm = pl.BlockSpec(memory_space=pltpu.HBM)
    packed = pl.pallas_call(
        pack_kernel,
        out_shape=jax.ShapeDtypeStruct((3 * fine, width), bf16),
        in_specs=[hbm] * 3,
        out_specs=vmem,
        scratch_shapes=[
            pltpu.VMEM((2, fine, width), left_image.dtype),
            pltpu.VMEM((fine, width), f32),
            pltpu.SemaphoreType.DMA((3,)),
        ],
        compiler_params=pltpu.CompilerParams(vmem_limit_bytes=2 * 2**20),
        name="pack",
    )(in_hbm(left_image), in_hbm(right_image), in_hbm(confidence))
    from_pair = lax.ppermute(packed, both, pairs)
    from_other = lax.ppermute(packed, both, others)

    groups = 6 * local_rows
    project, first, second, consts = pl.pallas_call(
        prepare_kernel,
        out_shape=(
            jax.ShapeDtypeStruct((3 * groups * CH, groups * UP * UP), bf16),
            jax.ShapeDtypeStruct((192, 256), bf16),
            jax.ShapeDtypeStruct((192, 256), bf16),
            jax.ShapeDtypeStruct((3, 64, cols), f32),
        ),
        in_specs=[vmem, vmem, vmem, hbm, vmem, vmem],
        out_specs=(vmem,) * 4,
        scratch_shapes=[
            pltpu.VMEM((1,) + first_weight.shape, bf16),
            pltpu.SemaphoreType.DMA((1,)),
        ],
        compiler_params=pltpu.CompilerParams(vmem_limit_bytes=8 * 2**20),
        name="prepare",
    )(
        feat_weight,
        first_weight,
        first_bias,
        in_hbm(second_weight),
        second_bias,
        head_weight,
    )
    total, left, conf = pl.pallas_call(
        functools.partial(score_kernel, pix_size=pix_size, disp_size=disp_size),
        out_shape=(
            jax.ShapeDtypeStruct((8, cols), f32),
            jax.ShapeDtypeStruct((3 * local_rows * CH, cols), bf16),
            jax.ShapeDtypeStruct((3 * fine, width), f32),
        ),
        in_specs=[vmem] * 7,
        out_specs=(vmem, vmem, vmem),
        scratch_shapes=[
            pltpu.VMEM((plane_count + 4, 3 * local_rows * CH, cols), bf16),
            pltpu.VMEM((plane_count + 2, (local_rows + 2) * CH, cols), bf16),
        ],
        compiler_params=pltpu.CompilerParams(vmem_limit_bytes=16 * 2**20),
        name="score",
    )(packed, from_pair, from_other, project, first, second, consts)

    total = total[:4]
    summed = total + lax.ppermute(total, "disp", swap)
    coarse = summed[local_rows:] / summed[:local_rows]
    received = lax.ppermute(coarse, both, neighbours)
    far_rows = lax.ppermute(coarse, both, far)
    exchanged = lax.ppermute(received, "disp", swap)
    swapped = lax.ppermute(far_rows, "disp", swap)
    mix = pl.pallas_call(
        mixing_kernel,
        out_shape=jax.ShapeDtypeStruct((3 * local_rows, mask_weight.shape[1], cols), f32),
        in_specs=[vmem, vmem],
        out_specs=vmem,
        compiler_params=pltpu.CompilerParams(vmem_limit_bytes=4 * 2**20),
        name="mixing",
    )(left, mask_weight)
    refined = pl.pallas_call(
        functools.partial(refine_kernel, pix_size=pix_size),
        out_shape=jax.ShapeDtypeStruct((fine, width), f32),
        in_specs=[vmem] * 7,
        out_specs=vmem,
        compiler_params=pltpu.CompilerParams(vmem_limit_bytes=8 * 2**20),
        name="refine",
    )(coarse, received, exchanged, far_rows, swapped, mix, conf)
    return (coarse, refined)


def solution(mesh):
    rows = P(("grp", "pix"), None)
    placed = (rows, rows, P(), P(), P(), P(), P(), P(), P(), rows)
    return jax.shard_map(
        functools.partial(local, pix_size=mesh.shape["pix"], disp_size=mesh.shape["disp"]),
        mesh=mesh,
        in_specs=placed,
        out_specs=(rows, rows),
        check_vma=False,
    )
```
